128 devices in a mesh: wide: 8 (over y, x_hi), narrow: 16 (over x_lo, z, core).
Axes of the slice: x: 4 (x_hi: 2, x_lo: 2; x = x_hi * 2 + x_lo), y: 4, z: 4, core: 2. Of those that a mesh axis runs over, the one named last changes fastest.
Arguments:
- tensor3: bfloat16 [512, 1024, 1024], P('wide', 'narrow'), may hold values from -6 to 6
- pattern: int32 [8, 16, 16], P('wide', 'narrow'), may hold values 0 or 1
- orbitals: bfloat16 [1024, 256], P('narrow'), may hold values from -0.01171875 to 0.01171875
- metric: bfloat16 [512, 512], replicated, may hold values from -1 to 2, as said below
Outputs:
- exchange_matrix: float32 [1024, 1024], P(('wide', 'narrow'))
The draws below stay inside these ranges and needn't reach their ends.
Inputs may be any that keep to these rules, and one draw needn't show every extreme that they name: metric is symmetric.
All inputs are finite; a program needn't handle non-finite values. No bound on the sum of `pattern` on one device may be relied on, other than what follows from the above.
Results may differ from the reference program's by a relative error of at most 0.0006.
Values may be sent and summed in bfloat16 or wider, within the bound.
No kernel may reach another device: no remote copies, remote signals or barrier semaphores. Data moves between devices by JAX's collectives and lax.ppermute only.
A program may use at most 128 MiB of HBM per device.

```python
import math
import jax
import jax.numpy as jnp
from jax import lax

BLK = 64
OCC = 256
RI = 512
NU = 1024


def draw_metric(key, part):
    entries = jnp.clip(jax.random.normal(key, (RI, RI), jnp.float32), -4.0, 4.0)
    coupling = (entries + entries.T) * (0.5 / math.sqrt(RI))
    identity = (lax.broadcasted_iota(jnp.int32, (RI, RI), 0) == lax.broadcasted_iota(jnp.int32, (RI, RI), 1)).astype(jnp.float32)
    return (coupling + identity).astype(jnp.bfloat16)


def place_ends(array, key, smallest, high):
    place = [jax.random.randint(jax.random.fold_in(key, axis), (), 0, length) for axis, length in enumerate(array.shape)]
    longest = array.shape.index(max(array.shape))
    next_to = place[:longest] + [(place[longest] + 1) % array.shape[longest]] + place[longest + 1:]
    return array.at[tuple(place)].set(smallest).at[tuple(next_to)].set(high)


def steps_of(key, extent, cuts, smallest, top_value):
    def one(position, parts):
        draws = jax.random.uniform(jax.random.fold_in(jax.random.fold_in(key, 6), position), (parts,), jnp.float32, smallest / len(cuts), top_value / len(cuts))
        return jnp.repeat(jnp.exp(draws), extent[position] // parts).reshape((-1,) + (1,) * (len(extent) - position - 1))

    loudness = one(*cuts[0])
    for cut in cuts[1:]:
        loudness = loudness * one(*cut)
    return loudness


def normal_values(key, dims, spread, most, shards=(), held_as=jnp.bfloat16):
    values = jax.random.normal(key, dims, jnp.float32) * spread
    if len(shards) > 0:
        values = steps_of(key, dims, shards, -0.22, 0.18) * values
    return jnp.clip(values, min=-most, max=most).astype(held_as)


def setup_inputs(seed: int = 0) -> dict:
    streams_of = jax.random.split(jax.random.key(seed), 5)
    return {
        "tensor3": normal_values(streams_of[0], (RI, NU, NU), 1.0, 6.0, ((0, 8), (1, 16))),
        "pattern": place_ends((jax.random.randint(streams_of[1], (RI // BLK, NU // BLK, NU // BLK), 0, 3) < 2).astype(jnp.int32), jax.random.fold_in(streams_of[1], 1), 0, 1),
        "orbitals": normal_values(streams_of[2], (NU, OCC), (NU * 256) ** -0.5, 0.01171875, ((0, 16),)),
        "metric": draw_metric(jax.random.fold_in(streams_of[4], 71), 0),
    }


def contract_block(inputs):
    tensor_block, block_mask = inputs
    cell_mask = jnp.repeat(jnp.repeat(block_mask, BLK, axis=0), BLK, axis=1).astype(jnp.bfloat16)
    masked = tensor_block * cell_mask[None]
    product = jnp.dot(masked.reshape(BLK * NU, NU), orbitals_global[0], preferred_element_type=jnp.float32)
    return product.astype(jnp.bfloat16).reshape(BLK, NU, OCC)


orbitals_global = []


def reference(tensor3, pattern, orbitals, metric):
    def contract_one(inputs):
        tensor_block, block_mask = inputs
        cell_mask = jnp.repeat(jnp.repeat(block_mask, BLK, axis=0), BLK, axis=1).astype(jnp.bfloat16)
        masked = tensor_block * cell_mask[None]
        product = jnp.dot(masked.reshape(BLK * NU, NU), orbitals, preferred_element_type=jnp.float32)
        return product.astype(jnp.bfloat16).reshape(BLK, NU, OCC)

    blocks = tensor3.reshape(RI // BLK, BLK, NU, NU)
    coeffs = lax.map(contract_one, (blocks, pattern)).reshape(RI, NU, OCC)
    fitted = jnp.dot(metric, coeffs.reshape(RI, NU * OCC), preferred_element_type=jnp.float32)
    fitted = fitted.astype(jnp.bfloat16).reshape(RI, NU, OCC)

    def accumulate(running, row_pair):
        fit_row, coef_row = row_pair
        return running - jnp.dot(fit_row, coef_row.T, preferred_element_type=jnp.float32), None

    exchange_matrix, unused = lax.scan(accumulate, jnp.zeros((NU, NU), jnp.float32), (fitted, coeffs))
    return exchange_matrix
```

```python
import jax
import jax.numpy as jnp
from jax import lax
from jax.sharding import PartitionSpec as P

BLK = 64
BOTH = ("wide", "narrow")


def body(tensor3, pattern, orbitals, metric):
    ri_local, ao_local, basis_all = tensor3.shape
    n_wide, n_narrow = lax.axis_size("wide"), lax.axis_size("narrow")
    devices = n_wide * n_narrow
    occupied = orbitals.shape[1]
    share = occupied // devices
    orbs = lax.all_to_all(
        jnp.broadcast_to(orbitals[None], (n_narrow, *orbitals.shape)), "narrow", 0, 0, tiled=True
    ).reshape(basis_all, occupied)
    mask = jnp.repeat(pattern.reshape(-1), BLK).astype(jnp.bfloat16)
    masked = (tensor3 * mask).reshape(ri_local * ao_local, basis_all)
    coeffs = jnp.dot(masked, orbs, preferred_element_type=jnp.float32).astype(jnp.bfloat16)
    parts = coeffs.reshape(ri_local, ao_local, share, devices).transpose(3, 1, 2, 0)
    parts = parts.reshape(devices, ao_local, share * ri_local)
    got = lax.all_to_all(parts, BOTH, 0, 0, tiled=True)
    lanes = share * ri_local
    coef = got.reshape(n_wide, n_narrow * ao_local, lanes).transpose(1, 0, 2)
    coef = coef.reshape(n_narrow * ao_local, n_wide * lanes)
    spread = metric.reshape(n_wide, 1, ri_local, n_wide, 1, ri_local)
    same = jnp.eye(share, dtype=metric.dtype).reshape(1, share, 1, 1, share, 1)
    spread = (spread * same).reshape(n_wide * lanes, n_wide * lanes)
    fitted = jnp.dot(coef, spread, preferred_element_type=jnp.float32).astype(jnp.bfloat16)
    term = lax.dot_general(
        fitted, coef, (((1,), (1,)), ((), ())), preferred_element_type=jnp.float32
    )
    rows = term.shape[0] // devices
    term = lax.all_to_all(term.reshape(devices, rows, -1), BOTH, 0, 0, tiled=True)
    return -jnp.sum(term, axis=0)


def solution(mesh):
    in_specs = (P("wide", "narrow", None), P("wide", "narrow", None), P("narrow", None), P())
    out_specs = P(("wide", "narrow"), None)
    return jax.shard_map(body, mesh=mesh, in_specs=in_specs, out_specs=out_specs, check_vma=False)
```

```python
import functools

import jax
import jax.numpy as jnp
from jax import lax
from jax.experimental import pallas as pl
from jax.experimental.pallas import tpu as pltpu
from jax.sharding import PartitionSpec as P

BLK = 64
BOTH = ("wide", "narrow")
BF16, F32 = jnp.bfloat16, jnp.float32
VMEM = pl.BlockSpec(memory_space=pltpu.VMEM)
SMEM = pl.BlockSpec(memory_space=pltpu.SMEM)
NT = (((1,), (1,)), ((), ()))
NN = (((1,), (0,)), ((), ()))


def params(mib):
    return pltpu.CompilerParams(vmem_limit_bytes=mib << 20)


def reorder_kernel(tensor_ref, rows_ref):
    block = tensor_ref[...]
    ri, step, basis = block.shape
    rows = pl.ds(pl.multiple_of(pl.program_id(0) * step * ri, step * ri), step * ri)
    rows_ref[rows, :] = pltpu.einshape("pmn->mpn", block).reshape(step * ri, basis)


def reorder(tensor3, step=16):
    ri, mu, basis = tensor3.shape
    return pl.pallas_call(
        reorder_kernel,
        out_shape=jax.ShapeDtypeStruct((mu * ri, basis), BF16),
        grid=(mu // step,),
        in_specs=[pl.BlockSpec((ri, step, basis), lambda s: (0, s, 0))],
        out_specs=VMEM,
        compiler_params=params(20),
        cost_estimate=pl.CostEstimate(flops=0, bytes_accessed=4 * tensor3.size, transcendentals=0),
        name="reorder",
    )(tensor3)


def coeffs_kernel(step, pattern_ref, orbs_ref, rows_ref, out_ref, masked, turned):
    for b in range(orbs_ref.shape[0] // BLK):
        rows = pl.ds(b * BLK, BLK)
        masked[rows, :] = orbs_ref[rows, :].astype(F32) * pattern_ref[b].astype(F32)
    turned[...] = masked[...].T.astype(BF16)
    owners, mu, lanes = out_ref.shape
    ri = lanes // 2
    low = lax.broadcasted_iota(jnp.int32, (owners, lanes), 1) < ri
    for s in range(mu // step):
        tile = rows_ref[s * step * ri : (s + 1) * step * ri]
        value = lax.dot_general(turned[...], tile, NT, preferred_element_type=F32)
        first, second = value[:owners], value[owners:]
        pieces = []
        for g in range(step // 2):
            x = first[:, g * lanes : (g + 1) * lanes]
            y = second[:, g * lanes : (g + 1) * lanes]
            pieces.append(jnp.where(low, x, pltpu.roll(y, ri, 1)))
            pieces.append(jnp.where(low, pltpu.roll(x, ri, 1), y))
        stacked = jnp.stack(pieces).astype(BF16)
        out_ref[:, s * step : (s + 1) * step, :] = pltpu.einshape("mjl->jml", stacked)


def coeffs_of(pattern, orbs, rows, ri, owners, step=16):
    basis, occupied = orbs.shape
    mu = rows.shape[0] // ri
    return pl.pallas_call(
        functools.partial(coeffs_kernel, step),
        out_shape=jax.ShapeDtypeStruct((owners, mu, 2 * ri), BF16),
        in_specs=[SMEM, VMEM, VMEM],
        out_specs=VMEM,
        scratch_shapes=[pltpu.VMEM((basis, occupied), F32), pltpu.VMEM((occupied, basis), BF16)],
        compiler_params=params(20),
        cost_estimate=pl.CostEstimate(
            flops=2 * rows.size * occupied, bytes_accessed=2 * rows.size, transcendentals=0
        ),
        name="coeffs",
    )(pattern, orbs, rows)


def spread_kernel(metric_ref, out_ref):
    ri = metric_ref.shape[0]
    low = lax.broadcasted_iota(jnp.int32, (BLK, 2 * BLK), 1) < BLK
    zero = jnp.zeros((BLK, 2 * BLK), F32)
    for w in range(ri // BLK):
        for g in range(ri // (2 * BLK)):
            x = metric_ref[w * BLK : (w + 1) * BLK, 2 * g * BLK : 2 * (g + 1) * BLK].astype(F32)
            y = pltpu.roll(x, BLK, 1)
            left, right = slice(4 * g * BLK, (4 * g + 2) * BLK), slice((4 * g + 2) * BLK, (4 * g + 4) * BLK)
            one, two = slice(2 * w * BLK, (2 * w + 1) * BLK), slice((2 * w + 1) * BLK, (2 * w + 2) * BLK)
            out_ref[one, left] = jnp.where(low, x, zero).astype(BF16)
            out_ref[one, right] = jnp.where(low, y, zero).astype(BF16)
            out_ref[two, left] = jnp.where(low, zero, y).astype(BF16)
            out_ref[two, right] = jnp.where(low, zero, x).astype(BF16)


def spread_of(metric):
    ri = metric.shape[0]
    return pl.pallas_call(
        spread_kernel,
        out_shape=jax.ShapeDtypeStruct((2 * ri, 2 * ri), BF16),
        in_specs=[VMEM],
        out_specs=VMEM,
        compiler_params=params(16),
        cost_estimate=pl.CostEstimate(flops=0, bytes_accessed=10 * metric.size, transcendentals=0),
        name="spread",
    )(metric)


def partial_term(core, coef_ref, spread_ref):
    wide, mu, lanes = coef_ref.shape
    coef = jnp.concatenate([coef_ref[w] for w in range(wide)], axis=1)
    mine = coef.astype(F32).reshape(mu // 16, 2, 8, wide * lanes)
    mine = jnp.where(core == 0, mine[:, 0], mine[:, 1]).reshape(mu // 2, wide * lanes)
    fitted = lax.dot_general(mine.astype(BF16), spread_ref[...], NN, preferred_element_type=F32)
    return lax.dot_general(fitted.astype(BF16), coef, NT, preferred_element_type=F32)


def own_kernel(core_ref, coef_ref, spread_ref, out_ref):
    out_ref[...] = partial_term(core_ref[0], coef_ref, spread_ref)


def other_kernel(core_ref, coef_ref, spread_ref, first_ref, out_ref):
    core = core_ref[0]
    term = first_ref[...] + partial_term(core, coef_ref, spread_ref)
    blocks, rows, columns = out_ref.shape
    term = term.reshape(blocks, rows, columns)
    largest = jnp.max(jnp.max(jnp.abs(term), axis=2, keepdims=True), axis=1, keepdims=True)
    power = jnp.floor(jnp.log2(jnp.maximum(largest, 1e-30))) - 13.0
    block = lax.broadcasted_iota(jnp.int32, (blocks, rows, columns), 0)
    row = lax.broadcasted_iota(jnp.int32, (blocks, rows, columns), 1)
    column = lax.broadcasted_iota(jnp.int32, (blocks, rows, columns), 2)
    spot = (row == rows - 1) & (column == rows * (2 * block + core))
    out_ref[...] = jnp.where(spot, power, term * jnp.exp2(-power))


def own_term(core, coef, spread):
    wide, mu, lanes = coef.shape
    flops = 2 * (mu // 2) * wide * lanes * (wide * lanes + mu)
    return pl.pallas_call(
        own_kernel,
        out_shape=jax.ShapeDtypeStruct((mu // 2, mu), F32),
        in_specs=[SMEM, VMEM, VMEM],
        out_specs=VMEM,
        compiler_params=params(24),
        cost_estimate=pl.CostEstimate(flops=flops, bytes_accessed=4 * coef.size, transcendentals=0),
        name="own_term",
    )(core, coef, spread)


def other_term(core, coef, spread, first, devices):
    wide, mu, lanes = coef.shape
    flops = 2 * (mu // 2) * wide * lanes * (wide * lanes + mu)
    return pl.pallas_call(
        other_kernel,
        out_shape=jax.ShapeDtypeStruct((devices // 2, mu // devices, mu), F32),
        in_specs=[SMEM, VMEM, VMEM, VMEM],
        out_specs=VMEM,
        compiler_params=params(24),
        cost_estimate=pl.CostEstimate(flops=flops, bytes_accessed=8 * coef.size, transcendentals=0),
        name="other_term",
    )(core, coef, spread, first)


def body(tensor3, pattern, orbitals, metric):
    ri_local, mu_local, basis = tensor3.shape
    n_wide, n_narrow = lax.axis_size("wide"), lax.axis_size("narrow")
    devices = n_wide * n_narrow
    occupied = orbitals.shape[1]
    me = lax.axis_index("wide") * n_narrow + lax.axis_index("narrow")
    core = (me % 2).astype(jnp.int32)
    orbs = lax.all_to_all(
        jnp.broadcast_to(orbitals[None], (n_narrow, *orbitals.shape)), "narrow", 0, 0, tiled=True
    ).reshape(basis, occupied)
    rows = reorder(tensor3)
    spread = spread_of(metric)
    parts = coeffs_of(pattern.reshape(-1), orbs, rows, ri_local, devices)
    coef = lax.all_to_all(parts, BOTH, 0, 0, tiled=True)
    coef = coef.reshape(n_wide, n_narrow * mu_local, 2 * ri_local)
    other = lax.ppermute(coef, "narrow", [(i, i ^ 1) for i in range(n_narrow)])
    first = own_term(core.reshape(1), coef, spread)
    scaled = other_term(core.reshape(1), other, spread, first, devices).astype(jnp.float16)
    sides = [[j for j in range(devices) if j % 2 == c] for c in (0, 1)]
    got = lax.all_to_all(scaled, BOTH, 0, 0, tiled=True, axis_index_groups=sides)
    blocks, height, _ = got.shape
    spot = me * height
    power = lax.dynamic_slice(got, (0, height - 1, spot), (blocks, 1, 1)).astype(F32)
    total = jnp.sum(got.astype(F32) * jnp.exp2(power), axis=0)
    mirrored = lax.dynamic_slice(total, (0, spot + height - 1), (1, 1))
    return -lax.dynamic_update_slice(total, mirrored, (height - 1, spot))


def solution(mesh):
    in_specs = (P("wide", "narrow", None), P("wide", "narrow", None), P("narrow", None), P())
    out_specs = P(("wide", "narrow"), None)
    return jax.shard_map(body, mesh=mesh, in_specs=in_specs, out_specs=out_specs, check_vma=False)
```

```python
import functools

import jax
import jax.numpy as jnp
from jax import lax
from jax.experimental import pallas as pl
from jax.experimental.pallas import tpu as pltpu
from jax.sharding import PartitionSpec as P

BLK = 64
BOTH = ("wide", "narrow")
BF16, F32 = jnp.bfloat16, jnp.float32
TOP = 32766.0
VMEM = pl.BlockSpec(memory_space=pltpu.VMEM)
SMEM = pl.BlockSpec(memory_space=pltpu.SMEM)
NT = (((1,), (1,)), ((), ()))


def params(mib):
    return pltpu.CompilerParams(vmem_limit_bytes=mib << 20)


def copies_kernel(orbitals_ref, out_ref):
    for i in range(out_ref.shape[0]):
        out_ref[i] = orbitals_ref[...]


def copies_of(orbitals, count):
    return pl.pallas_call(
        copies_kernel,
        out_shape=jax.ShapeDtypeStruct((count, *orbitals.shape), BF16),
        in_specs=[VMEM],
        out_specs=VMEM,
        compiler_params=params(8),
        name="copies",
    )(orbitals)


def reorder_kernel(tensor_ref, rows_ref):
    block = tensor_ref[...]
    ri, halves, step, basis = block.shape
    turned = jnp.stack([pltpu.einshape("pmn->mpn", block[:, h]) for h in range(halves)], axis=1)
    rows_ref[...] = turned.reshape(step * halves * ri, basis)


def reorder(tensor3, step=8):
    ri, mu, basis = tensor3.shape
    return pl.pallas_call(
        reorder_kernel,
        out_shape=jax.ShapeDtypeStruct((mu * ri, basis), BF16),
        grid=(mu // 2 // step,),
        in_specs=[pl.BlockSpec((ri, 2, step, basis), lambda s: (0, 0, s, 0))],
        out_specs=pl.BlockSpec((2 * step * ri, basis), lambda s: (s, 0)),
        compiler_params=params(48),
        cost_estimate=pl.CostEstimate(flops=0, bytes_accessed=4 * tensor3.size, transcendentals=0),
        name="reorder",
    )(tensor3.reshape(ri, 2, mu // 2, basis))


def coeffs_kernel(step, pattern_ref, orbs_ref, rows_ref, out_ref, masked, turned, tiles, sems):
    owners, height, lanes = out_ref.shape
    height //= 2
    span = step * lanes
    steps = height // step
    copies = [
        pltpu.make_async_copy(rows_ref.at[pl.ds(s * span, span)], tiles.at[s], sems.at[s])
        for s in range(steps)
    ]
    for copy in copies:
        copy.start()
    for b in range(orbs_ref.shape[0] // BLK):
        rows = pl.ds(b * BLK, BLK)
        masked[rows, :] = orbs_ref[rows, :].astype(F32) * pattern_ref[b].astype(F32)
    turned[...] = masked[...].T.astype(BF16)
    for s in range(steps):
        copies[s].wait()
        value = lax.dot_general(turned[...], tiles[s], NT, preferred_element_type=F32)
        for i in range(2):
            part = value[i * owners : (i + 1) * owners].astype(BF16)
            stacked = jnp.stack([part[:, g * lanes : (g + 1) * lanes] for g in range(step)])
            first = i * height + s * step
            out_ref[:, first : first + step, :] = pltpu.einshape("mjl->jml", stacked)


def coeffs_of(pattern, orbs, rows, ri, owners, step=8):
    basis, occupied = orbs.shape
    mu = rows.shape[0] // ri
    steps = mu // 2 // step
    return pl.pallas_call(
        functools.partial(coeffs_kernel, step),
        out_shape=jax.ShapeDtypeStruct((owners, mu, 2 * ri), BF16),
        in_specs=[SMEM, VMEM, pl.BlockSpec(memory_space=pltpu.HBM)],
        out_specs=VMEM,
        scratch_shapes=[
            pltpu.VMEM((basis, occupied), F32),
            pltpu.VMEM((occupied, basis), BF16),
            pltpu.VMEM((steps, step * 2 * ri, basis), BF16),
            pltpu.SemaphoreType.DMA((steps,)),
        ],
        compiler_params=params(56),
        cost_estimate=pl.CostEstimate(
            flops=2 * rows.size * occupied, bytes_accessed=2 * rows.size, transcendentals=0
        ),
        name="coeffs",
    )(pattern, orbs, rows)


def term_of(core, coef_ref, metric_ref):
    wide, blocks, orbitals, half, lanes = coef_ref.shape
    height = blocks * half
    width = wide * lanes // 2
    low = lax.broadcasted_iota(jnp.int32, (height, lanes), 1) < lanes // 2
    coefs, fits = [], []
    for i in range(orbitals):
        one, two = [], []
        for g in range(wide // 2):
            x = coef_ref[2 * g, :, i].reshape(height, lanes)
            y = coef_ref[2 * g + 1, :, i].reshape(height, lanes)
            one.append(jnp.where(low, x, pltpu.roll(y, lanes // 2, 1)))
            two.append(jnp.where(low, pltpu.roll(x, lanes // 2, 1), y))
        pair = [jnp.concatenate(v, axis=1).reshape(blocks, 1, half, width) for v in (one, two)]
        coef = jnp.concatenate(pair, axis=1).reshape(2 * height, width)
        mine = coef.astype(F32).reshape(height // 8, 2, 8, width)
        mine = jnp.where(core == 0, mine[:, 0], mine[:, 1]).reshape(height, width)
        fit = lax.dot_general(mine.astype(BF16), metric_ref[...], NT, preferred_element_type=F32)
        coefs.append(coef)
        fits.append(fit.astype(BF16))
    fit, coef = jnp.concatenate(fits, axis=1), jnp.concatenate(coefs, axis=1)
    return lax.dot_general(fit, coef, NT, preferred_element_type=F32)


def own_kernel(core_ref, coef_ref, metric_ref, out_ref):
    out_ref[...] = term_of(core_ref[0], coef_ref, metric_ref)


def last_kernel(core_ref, coef_ref, metric_ref, sum_ref, out_ref):
    core = core_ref[0]
    blocks, rows, columns = out_ref.shape
    term = (sum_ref[...] + term_of(core, coef_ref, metric_ref)).reshape(blocks, rows, columns)
    largest = jnp.max(jnp.abs(term), axis=2, keepdims=True)
    code = jnp.ceil(jnp.log2(jnp.maximum(largest, 1e-30)) * 256.0)
    scaled = term * (jnp.exp2(code * (-1.0 / 256.0)) * TOP)
    block = lax.broadcasted_iota(jnp.int32, (blocks, rows, columns), 0)
    row = lax.broadcasted_iota(jnp.int32, (blocks, rows, columns), 1)
    column = lax.broadcasted_iota(jnp.int32, (blocks, rows, columns), 2)
    column = column - rows * (2 * block + core)
    scaled = jnp.where((column == 0) & (row > 0), code, scaled)
    scaled = jnp.where((column == 1) & (row == rows - 1), code[:, 0:1], scaled)
    out_ref[...] = jnp.round(scaled).astype(jnp.int32).astype(jnp.int16)


def term_call(kernel, name, out_shape, core, *operands):
    coef = operands[0]
    width = coef.shape[0] * coef.shape[4] // 2
    height = coef.shape[1] * coef.shape[3]
    flops = 2 * coef.shape[2] * height * width * (width + 2 * height)
    return pl.pallas_call(
        kernel,
        out_shape=out_shape,
        in_specs=[SMEM] + [VMEM] * len(operands),
        out_specs=VMEM,
        compiler_params=params(32),
        cost_estimate=pl.CostEstimate(flops=flops, bytes_accessed=6 * coef.size, transcendentals=0),
        name=name,
    )(core, *operands)


def finish_kernel(me_ref, got_ref, out_ref):
    blocks, rows, columns = got_ref.shape
    lanes = 128
    start = rows * me_ref[0]
    base = pl.multiple_of(start // lanes * lanes, lanes)
    at = start - base
    window = got_ref[:, :, pl.ds(base, lanes)].astype(jnp.int32).astype(F32)
    lane = lax.broadcasted_iota(jnp.int32, window.shape, 2)
    row = lax.broadcasted_iota(jnp.int32, window.shape, 1)
    code = jnp.sum(jnp.where(lane == at, window, 0.0), axis=2, keepdims=True)
    other = jnp.sum(jnp.where(lane == at + 1, window, 0.0), axis=2, keepdims=True)
    code = jnp.where(row[:, :, :1] == 0, other[:, rows - 1 :], code)
    factor = jnp.exp2(code * (1.0 / 256.0)) * (-1.0 / TOP)
    total = jnp.zeros((rows, columns), F32)
    for s in range(blocks):
        total += got_ref[s].astype(jnp.int32).astype(F32) * factor[s]
    out_ref[...] = total
    part = out_ref[:, pl.ds(base, lanes)]
    lane = lax.broadcasted_iota(jnp.int32, part.shape, 1) - at
    row = lax.broadcasted_iota(jnp.int32, part.shape, 0)
    first = jnp.broadcast_to(part[0:1], part.shape)
    mirrored = jnp.sum(jnp.where(lane == row, first, 0.0), axis=1, keepdims=True)
    corner = jnp.sum(jnp.where((lane == rows - 1) & (row == 1), part, 0.0))
    part = jnp.where((lane == 0) & (row > 0), mirrored, part)
    out_ref[:, pl.ds(base, lanes)] = jnp.where((lane == 1) & (row == rows - 1), corner, part)


def finish(me, got):
    return pl.pallas_call(
        finish_kernel,
        out_shape=jax.ShapeDtypeStruct(got.shape[1:], F32),
        in_specs=[SMEM, VMEM],
        out_specs=VMEM,
        compiler_params=params(8),
        name="finish",
    )(me, got)


def body(tensor3, pattern, orbitals, metric):
    ri_local, mu_local, basis = tensor3.shape
    n_wide, n_narrow = lax.axis_size("wide"), lax.axis_size("narrow")
    devices = n_wide * n_narrow
    occupied = orbitals.shape[1]
    mu = n_narrow * mu_local
    me = (lax.axis_index("wide") * n_narrow + lax.axis_index("narrow")).astype(jnp.int32)
    core = (lax.axis_index("narrow") & 1).astype(jnp.int32).reshape(1)
    orbs = lax.all_to_all(copies_of(orbitals, n_narrow), "narrow", 0, 0, tiled=True)
    orbs = orbs.reshape(basis, occupied)
    rows = reorder(tensor3)
    parts = coeffs_of(pattern.reshape(-1), orbs, rows, ri_local, devices)
    coef = lax.all_to_all(parts, BOTH, 0, 0, tiled=True)
    coef = coef.reshape(n_wide, n_narrow, 2, mu_local // 2, 2 * ri_local)
    other = lax.ppermute(coef, "narrow", [(i, i ^ 1) for i in range(n_narrow)])
    shape = jax.ShapeDtypeStruct((mu // 2, mu), F32)
    total = term_call(own_kernel, "own_term", shape, core, coef, metric)
    shape = jax.ShapeDtypeStruct((devices // 2, mu // devices, mu), jnp.int16)
    parts = term_call(last_kernel, "last_term", shape, core, other, metric, total)
    sides = [[j for j in range(devices) if j % 2 == c] for c in (0, 1)]
    got = lax.all_to_all(parts, BOTH, 0, 0, tiled=True, axis_index_groups=sides)
    return finish(me.reshape(1), got)


def solution(mesh):
    in_specs = (P("wide", "narrow", None), P("wide", "narrow", None), P("narrow", None), P())
    out_specs = P(("wide", "narrow"), None)
    return jax.shard_map(body, mesh=mesh, in_specs=in_specs, out_specs=out_specs, check_vma=False)
```

```python
import functools

import jax
import jax.numpy as jnp
from jax import lax
from jax.experimental import pallas as pl
from jax.experimental.pallas import tpu as pltpu
from jax.sharding import PartitionSpec as P

BLK = 64
BOTH = ("wide", "narrow")
BF16, F32 = jnp.bfloat16, jnp.float32
TOP = 32766.0
VMEM = pl.BlockSpec(memory_space=pltpu.VMEM)
SMEM = pl.BlockSpec(memory_space=pltpu.SMEM)
NT = (((1,), (1,)), ((), ()))


def params(mib):
    return pltpu.CompilerParams(vmem_limit_bytes=mib << 20)


def copies_kernel(orbitals_ref, out_ref, sems):
    copies = [
        pltpu.make_async_copy(orbitals_ref, out_ref.at[i], sems.at[i])
        for i in range(out_ref.shape[0])
    ]
    for copy in copies:
        copy.start()
    for copy in copies:
        copy.wait()


def copies_of(orbitals, count):
    return pl.pallas_call(
        copies_kernel,
        out_shape=jax.ShapeDtypeStruct((count, *orbitals.shape), BF16),
        in_specs=[pl.BlockSpec(memory_space=pl.ANY)],
        out_specs=pl.BlockSpec(memory_space=pl.ANY),
        scratch_shapes=[pltpu.SemaphoreType.DMA((count,))],
        compiler_params=params(8),
        cost_estimate=pl.CostEstimate(flops=10**10, bytes_accessed=40 << 20, transcendentals=0),
        name="copies",
    )(orbitals)


def coeffs_kernel(step, pattern_ref, orbs_ref, tensor_ref, out_ref, masked, turned, tiles):
    owners, height, lanes = out_ref.shape
    height, ri = height // 2, lanes // 2
    steps = height // step

    def gather(s):
        for h in range(2):
            block = tensor_ref[:, h * height + s * step : h * height + (s + 1) * step, :]
            block = pltpu.einshape("pmn->mpn", block)
            for m in range(step):
                first = m * lanes + h * ri
                tiles[s % 2, first : first + ri, :] = block[m]

    gather(0)
    for b in range(orbs_ref.shape[0] // BLK):
        rows = pl.ds(b * BLK, BLK)
        masked[rows, :] = orbs_ref[rows, :].astype(F32) * pattern_ref[b].astype(F32)
    turned[...] = masked[...].T.astype(BF16)
    for s in range(steps):
        if s + 1 < steps:
            gather(s + 1)
        value = lax.dot_general(turned[...], tiles[s % 2], NT, preferred_element_type=F32)
        for i in range(2):
            part = value[i * owners : (i + 1) * owners].astype(BF16)
            stacked = jnp.stack([part[:, g * lanes : (g + 1) * lanes] for g in range(step)])
            first = i * height + s * step
            out_ref[:, first : first + step, :] = pltpu.einshape("mjl->jml", stacked)


def coeffs_of(pattern, orbs, tensor3, owners, step=8):
    basis, occupied = orbs.shape
    ri, mu, _ = tensor3.shape
    return pl.pallas_call(
        functools.partial(coeffs_kernel, step),
        out_shape=jax.ShapeDtypeStruct((owners, mu, 2 * ri), BF16),
        in_specs=[SMEM, VMEM, VMEM],
        out_specs=VMEM,
        scratch_shapes=[
            pltpu.VMEM((basis, occupied), F32),
            pltpu.VMEM((occupied, basis), BF16),
            pltpu.VMEM((2, step * 2 * ri, basis), BF16),
        ],
        compiler_params=params(20),
        cost_estimate=pl.CostEstimate(
            flops=2 * tensor3.size * occupied, bytes_accessed=2 * tensor3.size, transcendentals=0
        ),
        name="coeffs",
    )(pattern, orbs, tensor3)


def term_of(core, coef_ref, metric_ref):
    wide, blocks, orbitals, half, lanes = coef_ref.shape
    height = blocks * half
    width = wide * lanes // 2
    low = lax.broadcasted_iota(jnp.int32, (height, lanes), 1) < lanes // 2
    coefs, fits = [], []
    for i in range(orbitals):
        one, two = [], []
        for g in range(wide // 2):
            x = coef_ref[2 * g, :, i].reshape(height, lanes)
            y = coef_ref[2 * g + 1, :, i].reshape(height, lanes)
            one.append(jnp.where(low, x, pltpu.roll(y, lanes // 2, 1)))
            two.append(jnp.where(low, pltpu.roll(x, lanes // 2, 1), y))
        pair = [jnp.concatenate(v, axis=1).reshape(blocks, 1, half, width) for v in (one, two)]
        coef = jnp.concatenate(pair, axis=1).reshape(2 * height, width)
        mine = coef.astype(F32).reshape(height // 8, 2, 8, width)
        mine = jnp.where(core == 0, mine[:, 0], mine[:, 1]).reshape(height, width)
        fit = lax.dot_general(mine.astype(BF16), metric_ref[...], NT, preferred_element_type=F32)
        coefs.append(coef)
        fits.append(fit.astype(BF16))
    fit, coef = jnp.concatenate(fits, axis=1), jnp.concatenate(coefs, axis=1)
    return lax.dot_general(fit, coef, NT, preferred_element_type=F32)


def own_kernel(core_ref, coef_ref, metric_ref, out_ref):
    out_ref[...] = term_of(core_ref[0], coef_ref, metric_ref)


def last_kernel(core_ref, coef_ref, metric_ref, sum_ref, out_ref):
    core = core_ref[0]
    blocks, rows, columns = out_ref.shape
    term = (sum_ref[...] + term_of(core, coef_ref, metric_ref)).reshape(blocks, rows, columns)
    largest = jnp.max(jnp.abs(term), axis=2, keepdims=True)
    code = jnp.ceil(jnp.log2(jnp.maximum(largest, 1e-30)) * 256.0)
    factor = jnp.exp2(code * (-1.0 / 256.0)) * TOP
    lanes = 128
    group = lanes // (2 * rows)
    shape = (group, rows, lanes)
    block = lax.broadcasted_iota(jnp.int32, shape, 0)
    row = lax.broadcasted_iota(jnp.int32, shape, 1)
    column = lax.broadcasted_iota(jnp.int32, shape, 2) - rows * (2 * block + core)
    first = (column == 0) & (row > 0)
    second = (column == 1) & (row == rows - 1)
    for g in range(blocks // group):
        some = slice(g * group, (g + 1) * group)
        codes = code[some]
        scaled = term[some] * factor[some]
        part = scaled[:, :, g * lanes : (g + 1) * lanes]
        part = jnp.where(first, codes, jnp.where(second, codes[:, 0:1], part))
        scaled = [scaled[:, :, : g * lanes], part, scaled[:, :, (g + 1) * lanes :]]
        scaled = jnp.concatenate([piece for piece in scaled if piece.size], axis=2)
        out_ref[some] = jnp.round(scaled).astype(jnp.int32).astype(jnp.int16)


def term_call(kernel, name, out_shape, core, *operands):
    coef = operands[0]
    width = coef.shape[0] * coef.shape[4] // 2
    height = coef.shape[1] * coef.shape[3]
    flops = 2 * coef.shape[2] * height * width * (width + 2 * height)
    return pl.pallas_call(
        kernel,
        out_shape=out_shape,
        in_specs=[SMEM] + [VMEM] * len(operands),
        out_specs=VMEM,
        compiler_params=params(32),
        cost_estimate=pl.CostEstimate(flops=flops, bytes_accessed=6 * coef.size, transcendentals=0),
        name=name,
    )(core, *operands)


def finish_kernel(me_ref, got_ref, out_ref):
    blocks, rows, columns = got_ref.shape
    lanes = 128
    start = rows * me_ref[0]
    base = pl.multiple_of(start // lanes * lanes, lanes)
    at = start - base
    window = got_ref[:, :, pl.ds(base, lanes)].astype(jnp.int32).astype(F32)
    lane = lax.broadcasted_iota(jnp.int32, window.shape, 2)
    row = lax.broadcasted_iota(jnp.int32, window.shape, 1)
    code = jnp.sum(jnp.where(lane == at, window, 0.0), axis=2, keepdims=True)
    other = jnp.sum(jnp.where(lane == at + 1, window, 0.0), axis=2, keepdims=True)
    code = jnp.where(row[:, :, :1] == 0, other[:, rows - 1 :], code)
    factor = jnp.exp2(code * (1.0 / 256.0)) * (-1.0 / TOP)
    total = jnp.zeros((rows, columns), F32)
    for s in range(blocks):
        total += got_ref[s].astype(jnp.int32).astype(F32) * factor[s]
    out_ref[...] = total
    part = out_ref[:, pl.ds(base, lanes)]
    lane = lax.broadcasted_iota(jnp.int32, part.shape, 1) - at
    row = lax.broadcasted_iota(jnp.int32, part.shape, 0)
    first = jnp.broadcast_to(part[0:1], part.shape)
    mirrored = jnp.sum(jnp.where(lane == row, first, 0.0), axis=1, keepdims=True)
    corner = jnp.sum(jnp.where((lane == rows - 1) & (row == 1), part, 0.0))
    part = jnp.where((lane == 0) & (row > 0), mirrored, part)
    out_ref[:, pl.ds(base, lanes)] = jnp.where((lane == 1) & (row == rows - 1), corner, part)


def finish(me, got):
    return pl.pallas_call(
        finish_kernel,
        out_shape=jax.ShapeDtypeStruct(got.shape[1:], F32),
        in_specs=[SMEM, VMEM],
        out_specs=VMEM,
        compiler_params=params(8),
        name="finish",
    )(me, got)


def body(tensor3, pattern, orbitals, metric):
    ri_local, mu_local, basis = tensor3.shape
    n_wide, n_narrow = lax.axis_size("wide"), lax.axis_size("narrow")
    devices = n_wide * n_narrow
    occupied = orbitals.shape[1]
    mu = n_narrow * mu_local
    me = (lax.axis_index("wide") * n_narrow + lax.axis_index("narrow")).astype(jnp.int32)
    core = (lax.axis_index("narrow") & 1).astype(jnp.int32).reshape(1)
    orbs = lax.all_to_all(copies_of(orbitals, n_narrow), "narrow", 0, 0, tiled=True)
    orbs = orbs.reshape(basis, occupied)
    parts = coeffs_of(pattern.reshape(-1), orbs, tensor3, devices)
    coef = lax.all_to_all(parts, BOTH, 0, 0, tiled=True)
    coef = coef.reshape(n_wide, n_narrow, 2, mu_local // 2, 2 * ri_local)
    other = lax.ppermute(coef, "narrow", [(i, i ^ 1) for i in range(n_narrow)])
    shape = jax.ShapeDtypeStruct((mu // 2, mu), F32)
    total = term_call(own_kernel, "own_term", shape, core, coef, metric)
    shape = jax.ShapeDtypeStruct((devices // 2, mu // devices, mu), jnp.int16)
    parts = term_call(last_kernel, "last_term", shape, core, other, metric, total)
    sides = [[j for j in range(devices) if j % 2 == c] for c in (0, 1)]
    got = lax.all_to_all(parts, BOTH, 0, 0, tiled=True, axis_index_groups=sides)
    return finish(me.reshape(1), got)


def solution(mesh):
    in_specs = (P("wide", "narrow", None), P("wide", "narrow", None), P("narrow", None), P())
    out_specs = P(("wide", "narrow"), None)
    return jax.shard_map(body, mesh=mesh, in_specs=in_specs, out_specs=out_specs, check_vma=False)
```

```python
import functools

import jax
import jax.numpy as jnp
from jax import lax
from jax.experimental import pallas as pl
from jax.experimental.pallas import tpu as pltpu
from jax.sharding import PartitionSpec as P

BLK = 64
BOTH = ("wide", "narrow")
BF16, F32 = jnp.bfloat16, jnp.float32
TOP = 32766.0
VMEM = pl.BlockSpec(memory_space=pltpu.VMEM)
SMEM = pl.BlockSpec(memory_space=pltpu.SMEM)
NT = (((1,), (1,)), ((), ()))


def params(mib):
    return pltpu.CompilerParams(vmem_limit_bytes=mib << 20)


def copies_kernel(orbitals_ref, out_ref, sems):
    copies = [
        pltpu.make_async_copy(orbitals_ref, out_ref.at[i], sems.at[i])
        for i in range(out_ref.shape[0])
    ]
    for copy in copies:
        copy.start()
    for copy in copies:
        copy.wait()


def copies_of(orbitals, count):
    return pl.pallas_call(
        copies_kernel,
        out_shape=jax.ShapeDtypeStruct((count, *orbitals.shape), BF16),
        in_specs=[pl.BlockSpec(memory_space=pl.ANY)],
        out_specs=pl.BlockSpec(memory_space=pl.ANY),
        scratch_shapes=[pltpu.SemaphoreType.DMA((count,))],
        compiler_params=params(8),
        cost_estimate=pl.CostEstimate(flops=10**10, bytes_accessed=40 << 20, transcendentals=0),
        name="copies",
    )(orbitals)


def coeffs_kernel(step, pattern_ref, orbs_ref, tensor_ref, out_ref, masked):
    owners, height, lanes = out_ref.shape
    height, ri = height // 2, lanes // 2
    basis, occupied = orbs_ref.shape
    for b in range(basis // BLK):
        rows = pl.ds(b * BLK, BLK)
        masked[rows, :] = (orbs_ref[rows, :].astype(F32) * pattern_ref[b].astype(F32)).astype(BF16)
    for s in range(0, height, step):
        halves = []
        for h in range(2):
            block = tensor_ref[:, h * height + s : h * height + s + step, :]
            value = jnp.dot(
                block.reshape(ri * step, basis), masked[...], preferred_element_type=F32
            )
            halves.append(pltpu.einshape("pmi->mpi", value.reshape(ri, step, occupied)))
        value = jnp.concatenate(halves, axis=1)
        turned = jnp.stack([value[m].T for m in range(step)]).astype(BF16)
        turned = pltpu.einshape("mjl->jml", turned)
        for i in range(2):
            first = i * height + s
            out_ref[:, first : first + step, :] = turned[i * owners : (i + 1) * owners]


def coeffs_of(pattern, orbs, tensor3, owners, step=8):
    basis, occupied = orbs.shape
    ri, mu, _ = tensor3.shape
    return pl.pallas_call(
        functools.partial(coeffs_kernel, step),
        out_shape=jax.ShapeDtypeStruct((owners, mu, 2 * ri), BF16),
        in_specs=[SMEM, VMEM, VMEM],
        out_specs=VMEM,
        scratch_shapes=[pltpu.VMEM((basis, occupied), BF16)],
        compiler_params=params(20),
        cost_estimate=pl.CostEstimate(
            flops=2 * tensor3.size * occupied, bytes_accessed=2 * tensor3.size, transcendentals=0
        ),
        name="coeffs",
    )(pattern, orbs, tensor3)


def pack(coef_ref, out_ref):
    wide, blocks, orbitals, half, lanes = coef_ref.shape
    height, width = blocks * half, wide * lanes // 2
    low = lax.broadcasted_iota(jnp.int32, (height, lanes), 1) < lanes // 2
    for i in range(orbitals):
        for g in range(wide // 2):
            x = coef_ref[2 * g, :, i].reshape(height, lanes)
            y = coef_ref[2 * g + 1, :, i].reshape(height, lanes)
            one = jnp.where(low, x, pltpu.roll(y, lanes // 2, 1)).reshape(blocks, 1, half, lanes)
            two = jnp.where(low, pltpu.roll(x, lanes // 2, 1), y).reshape(blocks, 1, half, lanes)
            at = i * width + g * lanes
            both = jnp.concatenate([one, two], axis=1).reshape(2 * height, lanes)
            out_ref[:, at : at + lanes] = both


def term_of(core, first, count, packed_ref, metric_ref):
    width = metric_ref.shape[0]
    orbitals = packed_ref.shape[1] // width
    mine = packed_ref[first : first + count, :].astype(F32)
    mine = mine.reshape(count // 16, 2, 8, orbitals * width)
    mine = jnp.where(core == 0, mine[:, 0], mine[:, 1]).reshape(count // 2, orbitals * width)
    mine = mine.astype(BF16)
    fits = [
        lax.dot_general(
            mine[:, i * width : (i + 1) * width], metric_ref[...], NT, preferred_element_type=F32
        ).astype(BF16)
        for i in range(orbitals)
    ]
    fit = jnp.concatenate(fits, axis=1)
    return lax.dot_general(fit, packed_ref[...], NT, preferred_element_type=F32)


def first_kernel(core_ref, coef_ref, metric_ref, packed_ref, out_ref):
    pack(coef_ref, packed_ref)
    count = packed_ref.shape[0] // 2
    out_ref[...] = term_of(1 - core_ref[0], 0, count, packed_ref, metric_ref)


def second_kernel(core_ref, packed_ref, metric_ref, out_ref):
    count = packed_ref.shape[0] // 2
    out_ref[...] = term_of(1 - core_ref[0], count, count, packed_ref, metric_ref)


def own_kernel(core_ref, packed_ref, metric_ref, out_ref):
    out_ref[...] = term_of(core_ref[0], 0, packed_ref.shape[0], packed_ref, metric_ref)


def term_call(kernel, name, out_shape, core, *operands):
    rows = jax.tree.leaves(out_shape)[-1].shape[0]
    coef, metric = operands
    width = metric.shape[0]
    flops = 4 * rows * width * (width + coef.size // (2 * width))
    return pl.pallas_call(
        kernel,
        out_shape=out_shape,
        in_specs=[SMEM, VMEM, VMEM],
        out_specs=jax.tree.map(lambda _: VMEM, out_shape),
        compiler_params=params(20),
        cost_estimate=pl.CostEstimate(flops=flops, bytes_accessed=6 << 20, transcendentals=0),
        name=name,
    )(core, coef, metric)


def code_kernel(core_ref, sum_ref, one_ref, two_ref, out_ref, held, sems):
    copies = [
        pltpu.make_async_copy(ref, held.at[k], sems.at[k]) for k, ref in enumerate((one_ref, two_ref))
    ]
    for copy in copies:
        copy.start()
    core = core_ref[0]
    blocks, rows, columns = out_ref.shape
    lanes = 128
    group = lanes // (2 * rows)
    shape = (group, rows, lanes)
    block = lax.broadcasted_iota(jnp.int32, shape, 0)
    row = lax.broadcasted_iota(jnp.int32, shape, 1)
    column = lax.broadcasted_iota(jnp.int32, shape, 2) - rows * (2 * block + core)
    first = (column == 0) & (row > 0)
    second = (column == 1) & (row == rows - 1)
    groups = blocks // group
    for g in range(groups):
        k, at = divmod(g, groups // 2)
        if at == 0:
            copies[k].wait()
        term = sum_ref[g * group * rows : (g + 1) * group * rows, :]
        term += held[k, at * group * rows : (at + 1) * group * rows, :]
        term = term.reshape(group, rows, columns)
        largest = jnp.max(jnp.abs(term), axis=2, keepdims=True)
        code = jnp.ceil(jnp.log2(jnp.maximum(largest, 1e-30)) * 256.0)
        scaled = term * (jnp.exp2(code * (-1.0 / 256.0)) * TOP)
        part = scaled[:, :, g * lanes : (g + 1) * lanes]
        part = jnp.where(first, code, jnp.where(second, code[:, 0:1], part))
        scaled = [scaled[:, :, : g * lanes], part, scaled[:, :, (g + 1) * lanes :]]
        scaled = jnp.concatenate([piece for piece in scaled if piece.size], axis=2)
        out_ref[g * group : (g + 1) * group] = jnp.round(scaled).astype(jnp.int32).astype(jnp.int16)


def code_of(core, total, one, two, blocks):
    rows, columns = total.shape
    anywhere = pl.BlockSpec(memory_space=pl.ANY)
    return pl.pallas_call(
        code_kernel,
        out_shape=jax.ShapeDtypeStruct((blocks, rows // blocks, columns), jnp.int16),
        in_specs=[SMEM, VMEM, anywhere, anywhere],
        out_specs=VMEM,
        scratch_shapes=[pltpu.VMEM((2, *one.shape), F32), pltpu.SemaphoreType.DMA((2,))],
        compiler_params=params(16),
        cost_estimate=pl.CostEstimate(flops=0, bytes_accessed=6 << 20, transcendentals=0),
        name="code",
    )(core, total, one, two)


def finish_kernel(me_ref, got_ref, out_ref):
    blocks, rows, columns = got_ref.shape
    lanes = 128
    start = rows * me_ref[0]
    base = pl.multiple_of(start // lanes * lanes, lanes)
    at = start - base
    window = got_ref[:, :, pl.ds(base, lanes)].astype(jnp.int32).astype(F32)
    lane = lax.broadcasted_iota(jnp.int32, window.shape, 2)
    row = lax.broadcasted_iota(jnp.int32, window.shape, 1)
    code = jnp.sum(jnp.where(lane == at, window, 0.0), axis=2, keepdims=True)
    other = jnp.sum(jnp.where(lane == at + 1, window, 0.0), axis=2, keepdims=True)
    code = jnp.where(row[:, :, :1] == 0, other[:, rows - 1 :], code)
    factor = jnp.exp2(code * (1.0 / 256.0)) * (-1.0 / TOP)
    total = jnp.zeros((rows, columns), F32)
    for s in range(blocks):
        total += got_ref[s].astype(jnp.int32).astype(F32) * factor[s]
    out_ref[...] = total
    part = out_ref[:, pl.ds(base, lanes)]
    lane = lax.broadcasted_iota(jnp.int32, part.shape, 1) - at
    row = lax.broadcasted_iota(jnp.int32, part.shape, 0)
    first = jnp.broadcast_to(part[0:1], part.shape)
    mirrored = jnp.sum(jnp.where(lane == row, first, 0.0), axis=1, keepdims=True)
    corner = jnp.sum(jnp.where((lane == rows - 1) & (row == 1), part, 0.0))
    part = jnp.where((lane == 0) & (row > 0), mirrored, part)
    out_ref[:, pl.ds(base, lanes)] = jnp.where((lane == 1) & (row == rows - 1), corner, part)


def finish(me, got):
    return pl.pallas_call(
        finish_kernel,
        out_shape=jax.ShapeDtypeStruct(got.shape[1:], F32),
        in_specs=[SMEM, VMEM],
        out_specs=VMEM,
        compiler_params=params(8),
        name="finish",
    )(me, got)


def body(tensor3, pattern, orbitals, metric):
    ri_local, mu_local, basis = tensor3.shape
    n_wide, n_narrow = lax.axis_size("wide"), lax.axis_size("narrow")
    devices = n_wide * n_narrow
    me = (lax.axis_index("wide") * n_narrow + lax.axis_index("narrow")).astype(jnp.int32)
    core = (lax.axis_index("narrow") & 1).astype(jnp.int32).reshape(1)
    me, core, orbitals = lax.optimization_barrier((me.reshape(1), core, orbitals))
    swap = [(i, i ^ 1) for i in range(n_narrow)]
    orbs = lax.all_to_all(copies_of(orbitals, n_narrow), "narrow", 0, 0, tiled=True)
    orbs = orbs.reshape(basis, orbitals.shape[1])
    parts = coeffs_of(pattern.reshape(-1), orbs, tensor3, devices)
    coef = lax.all_to_all(parts, BOTH, 0, 0, tiled=True)
    coef = coef.reshape(n_wide, n_narrow, 2, mu_local // 2, 2 * ri_local)
    mu = n_narrow * mu_local
    quarter = jax.ShapeDtypeStruct((mu // 4, mu), F32)
    packed = jax.ShapeDtypeStruct((mu, 2 * metric.shape[0]), BF16)
    packed, one = term_call(first_kernel, "first", (packed, quarter), core, coef, metric)
    one = lax.ppermute(one, "narrow", swap)
    two = term_call(second_kernel, "second", quarter, core, packed, metric)
    two = lax.ppermute(two, "narrow", swap)
    total = jax.ShapeDtypeStruct((mu // 2, mu), F32)
    total = term_call(own_kernel, "own", total, core, packed, metric)
    parts = code_of(core, total, one, two, devices // 2)
    sides = [[j for j in range(devices) if j % 2 == c] for c in (0, 1)]
    got = lax.all_to_all(parts, BOTH, 0, 0, tiled=True, axis_index_groups=sides)
    return finish(me, got)


def solution(mesh):
    in_specs = (P("wide", "narrow", None), P("wide", "narrow", None), P("narrow", None), P())
    out_specs = P(("wide", "narrow"), None)
    return jax.shard_map(body, mesh=mesh, in_specs=in_specs, out_specs=out_specs, check_vma=False)
```

```python
import functools

import jax
import jax.numpy as jnp
from jax import lax
from jax.experimental import pallas as pl
from jax.experimental.pallas import tpu as pltpu
from jax.sharding import PartitionSpec as P

BLK = 64
BOTH = ("wide", "narrow")
BF16, F32 = jnp.bfloat16, jnp.float32
TOP = 32766.0
VMEM = pl.BlockSpec(memory_space=pltpu.VMEM)
SMEM = pl.BlockSpec(memory_space=pltpu.SMEM)
NT = (((1,), (1,)), ((), ()))


def params(mib):
    return pltpu.CompilerParams(vmem_limit_bytes=mib << 20)


def copies_kernel(orbitals_ref, out_ref, sems):
    copies = [
        pltpu.make_async_copy(orbitals_ref, out_ref.at[i], sems.at[i])
        for i in range(out_ref.shape[0])
    ]
    for copy in copies:
        copy.start()
    for copy in copies:
        copy.wait()


def copies_of(orbitals, count):
    return pl.pallas_call(
        copies_kernel,
        out_shape=jax.ShapeDtypeStruct((count, *orbitals.shape), BF16),
        in_specs=[pl.BlockSpec(memory_space=pl.ANY)],
        out_specs=pl.BlockSpec(memory_space=pl.ANY),
        scratch_shapes=[pltpu.SemaphoreType.DMA((count,))],
        compiler_params=params(8),
        cost_estimate=pl.CostEstimate(flops=10**10, bytes_accessed=40 << 20, transcendentals=0),
        name="copies",
    )(orbitals)


def coeffs_kernel(step, pattern_ref, orbs_ref, tensor_ref, out_ref, masked):
    owners, height, lanes = out_ref.shape
    height, ri = height // 2, lanes // 2
    basis, occupied = orbs_ref.shape
    for b in range(basis // BLK):
        rows = pl.ds(b * BLK, BLK)
        masked[rows, :] = (orbs_ref[rows, :].astype(F32) * pattern_ref[b].astype(F32)).astype(BF16)
    for s in range(0, height, step):
        halves = []
        for h in range(2):
            block = tensor_ref[:, h * height + s : h * height + s + step, :]
            value = jnp.dot(
                block.reshape(ri * step, basis), masked[...], preferred_element_type=F32
            )
            halves.append(pltpu.einshape("pmi->mpi", value.reshape(ri, step, occupied)))
        value = jnp.concatenate(halves, axis=1)
        turned = jnp.stack([value[m].T for m in range(step)]).astype(BF16)
        turned = pltpu.einshape("mjl->jml", turned)
        for i in range(2):
            first = i * height + s
            out_ref[:, first : first + step, :] = turned[i * owners : (i + 1) * owners]


def coeffs_of(pattern, orbs, tensor3, owners, step=8):
    basis, occupied = orbs.shape
    ri, mu, _ = tensor3.shape
    return pl.pallas_call(
        functools.partial(coeffs_kernel, step),
        out_shape=jax.ShapeDtypeStruct((owners, mu, 2 * ri), BF16),
        in_specs=[SMEM, VMEM, VMEM],
        out_specs=VMEM,
        scratch_shapes=[pltpu.VMEM((basis, occupied), BF16)],
        compiler_params=params(20),
        cost_estimate=pl.CostEstimate(
            flops=2 * tensor3.size * occupied, bytes_accessed=2 * tensor3.size, transcendentals=0
        ),
        name="coeffs",
    )(pattern, orbs, tensor3)


def pack(coef_ref, out_ref):
    wide, blocks, orbitals, half, lanes = coef_ref.shape
    height, width = blocks * half, wide * lanes // 2
    low = lax.broadcasted_iota(jnp.int32, (height, lanes), 1) < lanes // 2
    for i in range(orbitals):
        for g in range(wide // 2):
            x = coef_ref[2 * g, :, i].reshape(height, lanes)
            y = coef_ref[2 * g + 1, :, i].reshape(height, lanes)
            one = jnp.where(low, x, pltpu.roll(y, lanes // 2, 1)).reshape(blocks, 1, half, lanes)
            two = jnp.where(low, pltpu.roll(x, lanes // 2, 1), y).reshape(blocks, 1, half, lanes)
            at = i * width + g * lanes
            both = jnp.concatenate([one, two], axis=1).reshape(2 * height, lanes)
            out_ref[:, at : at + lanes] = both


def term_of(core, first, count, packed_ref, metric_ref):
    width = metric_ref.shape[0]
    orbitals = packed_ref.shape[1] // width
    mine = packed_ref[first : first + count, :].astype(F32)
    mine = mine.reshape(count // 16, 2, 8, orbitals * width)
    mine = jnp.where(core == 0, mine[:, 0], mine[:, 1]).reshape(count // 2, orbitals * width)
    mine = mine.astype(BF16)
    fits = [
        lax.dot_general(
            mine[:, i * width : (i + 1) * width], metric_ref[...], NT, preferred_element_type=F32
        ).astype(BF16)
        for i in range(orbitals)
    ]
    fit = jnp.concatenate(fits, axis=1)
    return lax.dot_general(fit, packed_ref[...], NT, preferred_element_type=F32)


def partner_kernel(core_ref, coef_ref, metric_ref, packed_ref, *out_refs):
    pack(coef_ref, packed_ref)
    term = term_of(1 - core_ref[0], 0, packed_ref.shape[0], packed_ref, metric_ref)
    rows = out_refs[0].shape[0]
    for k, out_ref in enumerate(out_refs):
        out_ref[...] = term[k * rows : (k + 1) * rows]


def own_kernel(core_ref, packed_ref, metric_ref, out_ref):
    out_ref[...] = term_of(core_ref[0], 0, packed_ref.shape[0], packed_ref, metric_ref)


def term_call(kernel, name, out_shape, core, coef, metric):
    width = metric.shape[0]
    columns = coef.size // (2 * width)
    flops = 2 * columns * width * (width + columns)
    return pl.pallas_call(
        kernel,
        out_shape=out_shape,
        in_specs=[SMEM, VMEM, VMEM],
        out_specs=jax.tree.map(lambda _: VMEM, out_shape),
        compiler_params=params(20),
        cost_estimate=pl.CostEstimate(flops=flops, bytes_accessed=6 << 20, transcendentals=0),
        name=name,
    )(core, coef, metric)


def code_kernel(core_ref, sum_ref, *refs):
    *part_refs, out_ref, held, sems = refs
    copies = [
        pltpu.make_async_copy(ref, held.at[k], sems.at[k]) for k, ref in enumerate(part_refs)
    ]
    for copy in copies:
        copy.start()
    core = core_ref[0]
    blocks, rows, columns = out_ref.shape
    lanes = 128
    group = lanes // (2 * rows)
    shape = (group, rows, lanes)
    block = lax.broadcasted_iota(jnp.int32, shape, 0)
    row = lax.broadcasted_iota(jnp.int32, shape, 1)
    column = lax.broadcasted_iota(jnp.int32, shape, 2) - rows * (2 * block + core)
    first = (column == 0) & (row > 0)
    second = (column == 1) & (row == rows - 1)
    groups = blocks // group
    for g in range(groups):
        k, at = divmod(g, groups // len(copies))
        if at == 0:
            copies[k].wait()
        term = sum_ref[g * group * rows : (g + 1) * group * rows, :]
        term += held[k, at * group * rows : (at + 1) * group * rows, :]
        term = term.reshape(group, rows, columns)
        largest = jnp.max(jnp.abs(term), axis=2, keepdims=True)
        code = jnp.ceil(jnp.log2(jnp.maximum(largest, 1e-30)) * 256.0)
        scaled = term * (jnp.exp2(code * (-1.0 / 256.0)) * TOP)
        part = scaled[:, :, g * lanes : (g + 1) * lanes]
        part = jnp.where(first, code, jnp.where(second, code[:, 0:1], part))
        scaled = [scaled[:, :, : g * lanes], part, scaled[:, :, (g + 1) * lanes :]]
        scaled = jnp.concatenate([piece for piece in scaled if piece.size], axis=2)
        out_ref[g * group : (g + 1) * group] = jnp.round(scaled).astype(jnp.int32).astype(jnp.int16)


def code_of(core, total, parts, blocks):
    rows, columns = total.shape
    count = len(parts)
    return pl.pallas_call(
        code_kernel,
        out_shape=jax.ShapeDtypeStruct((blocks, rows // blocks, columns), jnp.int16),
        in_specs=[SMEM, VMEM] + [pl.BlockSpec(memory_space=pl.ANY)] * count,
        out_specs=VMEM,
        scratch_shapes=[
            pltpu.VMEM((count, *parts[0].shape), F32),
            pltpu.SemaphoreType.DMA((count,)),
        ],
        compiler_params=params(16),
        cost_estimate=pl.CostEstimate(flops=0, bytes_accessed=6 << 20, transcendentals=0),
        name="code",
    )(core, total, *parts)


def finish_kernel(me_ref, got_ref, out_ref):
    blocks, rows, columns = got_ref.shape
    lanes = 128
    start = rows * me_ref[0]
    base = pl.multiple_of(start // lanes * lanes, lanes)
    at = start - base
    window = got_ref[:, :, pl.ds(base, lanes)].astype(jnp.int32).astype(F32)
    lane = lax.broadcasted_iota(jnp.int32, window.shape, 2)
    row = lax.broadcasted_iota(jnp.int32, window.shape, 1)
    code = jnp.sum(jnp.where(lane == at, window, 0.0), axis=2, keepdims=True)
    other = jnp.sum(jnp.where(lane == at + 1, window, 0.0), axis=2, keepdims=True)
    code = jnp.where(row[:, :, :1] == 0, other[:, rows - 1 :], code)
    factor = jnp.exp2(code * (1.0 / 256.0)) * (-1.0 / TOP)
    total = jnp.zeros((rows, columns), F32)
    for s in range(blocks):
        total += got_ref[s].astype(jnp.int32).astype(F32) * factor[s]
    out_ref[...] = total
    part = out_ref[:, pl.ds(base, lanes)]
    lane = lax.broadcasted_iota(jnp.int32, part.shape, 1) - at
    row = lax.broadcasted_iota(jnp.int32, part.shape, 0)
    first = jnp.broadcast_to(part[0:1], part.shape)
    mirrored = jnp.sum(jnp.where(lane == row, first, 0.0), axis=1, keepdims=True)
    corner = jnp.sum(jnp.where((lane == rows - 1) & (row == 1), part, 0.0))
    part = jnp.where((lane == 0) & (row > 0), mirrored, part)
    out_ref[:, pl.ds(base, lanes)] = jnp.where((lane == 1) & (row == rows - 1), corner, part)


def finish(me, got):
    return pl.pallas_call(
        finish_kernel,
        out_shape=jax.ShapeDtypeStruct(got.shape[1:], F32),
        in_specs=[SMEM, VMEM],
        out_specs=VMEM,
        compiler_params=params(8),
        name="finish",
    )(me, got)


def body(tensor3, pattern, orbitals, metric):
    ri_local, mu_local, basis = tensor3.shape
    n_wide, n_narrow = lax.axis_size("wide"), lax.axis_size("narrow")
    devices = n_wide * n_narrow
    me = (lax.axis_index("wide") * n_narrow + lax.axis_index("narrow")).astype(jnp.int32)
    core = (lax.axis_index("narrow") & 1).astype(jnp.int32).reshape(1)
    me, core, orbitals = lax.optimization_barrier((me.reshape(1), core, orbitals))
    swap = [(i, i ^ 1) for i in range(n_narrow)]
    orbs = lax.all_to_all(copies_of(orbitals, n_narrow), "narrow", 0, 0, tiled=True)
    orbs = orbs.reshape(basis, orbitals.shape[1])
    parts = coeffs_of(pattern.reshape(-1), orbs, tensor3, devices)
    coef = lax.all_to_all(parts, BOTH, 0, 0, tiled=True)
    coef = coef.reshape(n_wide, n_narrow, 2, mu_local // 2, 2 * ri_local)
    mu = n_narrow * mu_local
    packed = jax.ShapeDtypeStruct((mu, 2 * metric.shape[0]), BF16)
    part = jax.ShapeDtypeStruct((mu // 8, mu), F32)
    packed, *parts = term_call(partner_kernel, "partner", (packed,) + (part,) * 4, core, coef, metric)
    parts = [lax.ppermute(part, "narrow", swap) for part in parts]
    total = jax.ShapeDtypeStruct((mu // 2, mu), F32)
    total = term_call(own_kernel, "own", total, core, packed, metric)
    parts = code_of(core, total, parts, devices // 2)
    sides = [[j for j in range(devices) if j % 2 == c] for c in (0, 1)]
    got = lax.all_to_all(parts, BOTH, 0, 0, tiled=True, axis_index_groups=sides)
    return finish(me, got)


def solution(mesh):
    in_specs = (P("wide", "narrow", None), P("wide", "narrow", None), P("narrow", None), P())
    out_specs = P(("wide", "narrow"), None)
    return jax.shard_map(body, mesh=mesh, in_specs=in_specs, out_specs=out_specs, check_vma=False)
```

```python
import functools

import jax
import jax.numpy as jnp
from jax import lax
from jax.experimental import pallas as pl
from jax.experimental.pallas import tpu as pltpu
from jax.sharding import PartitionSpec as P

BLK = 64
BOTH = ("wide", "narrow")
BF16, F32 = jnp.bfloat16, jnp.float32
TOP = 32766.0
VMEM = pl.BlockSpec(memory_space=pltpu.VMEM)
SMEM = pl.BlockSpec(memory_space=pltpu.SMEM)
NT = (((1,), (1,)), ((), ()))


def params(mib):
    return pltpu.CompilerParams(vmem_limit_bytes=mib << 20)


def copies_kernel(orbitals_ref, out_ref, sems):
    copies = [
        pltpu.make_async_copy(orbitals_ref, out_ref.at[i], sems.at[i])
        for i in range(out_ref.shape[0])
    ]
    for copy in copies:
        copy.start()
    for copy in copies:
        copy.wait()


def copies_of(orbitals, count):
    return pl.pallas_call(
        copies_kernel,
        out_shape=jax.ShapeDtypeStruct((count, *orbitals.shape), BF16),
        in_specs=[pl.BlockSpec(memory_space=pl.ANY)],
        out_specs=pl.BlockSpec(memory_space=pl.ANY),
        scratch_shapes=[pltpu.SemaphoreType.DMA((count,))],
        compiler_params=params(8),
        cost_estimate=pl.CostEstimate(flops=10**10, bytes_accessed=40 << 20, transcendentals=0),
        name="copies",
    )(pltpu.with_memory_space_constraint(orbitals, pltpu.HBM))


def coeffs_kernel(step, pattern_ref, orbs_ref, tensor_ref, out_ref, masked):
    owners, height, lanes = out_ref.shape
    height, ri = height // 2, lanes // 2
    basis, occupied = orbs_ref.shape
    for b in range(basis // BLK):
        rows = pl.ds(b * BLK, BLK)
        masked[rows, :] = (orbs_ref[rows, :].astype(F32) * pattern_ref[b].astype(F32)).astype(BF16)
    for s in range(0, height, step):
        halves = []
        for h in range(2):
            block = tensor_ref[:, h * height + s : h * height + s + step, :]
            value = jnp.dot(
                block.reshape(ri * step, basis), masked[...], preferred_element_type=F32
            )
            value = value.astype(BF16).reshape(ri, step, occupied)
            halves.append(pltpu.einshape("pmi->mpi", value))
        value = jnp.concatenate(halves, axis=1)
        turned = jnp.stack([value[m].T for m in range(step)])
        turned = pltpu.einshape("mjl->jml", turned)
        for i in range(2):
            first = i * height + s
            out_ref[:, first : first + step, :] = turned[i * owners : (i + 1) * owners]


def coeffs_of(pattern, orbs, tensor3, owners, step=8):
    basis, occupied = orbs.shape
    ri, mu, _ = tensor3.shape
    return pl.pallas_call(
        functools.partial(coeffs_kernel, step),
        out_shape=jax.ShapeDtypeStruct((owners, mu, 2 * ri), BF16),
        in_specs=[SMEM, VMEM, VMEM],
        out_specs=VMEM,
        scratch_shapes=[pltpu.VMEM((basis, occupied), BF16)],
        compiler_params=params(20),
        cost_estimate=pl.CostEstimate(
            flops=2 * tensor3.size * occupied, bytes_accessed=2 * tensor3.size, transcendentals=0
        ),
        name="coeffs",
    )(pattern, orbs, tensor3)


def pack(coef_ref, out_ref):
    wide, blocks, orbitals, half, lanes = coef_ref.shape
    height, width = blocks * half, wide * lanes // 2
    low = lax.broadcasted_iota(jnp.int32, (height, lanes), 1) < lanes // 2
    for i in range(orbitals):
        for g in range(wide // 2):
            x = coef_ref[2 * g, :, i].reshape(height, lanes)
            y = coef_ref[2 * g + 1, :, i].reshape(height, lanes)
            one = jnp.where(low, x, pltpu.roll(y, lanes // 2, 1)).reshape(blocks, 1, half, lanes)
            two = jnp.where(low, pltpu.roll(x, lanes // 2, 1), y).reshape(blocks, 1, half, lanes)
            at = i * width + g * lanes
            both = jnp.concatenate([one, two], axis=1).reshape(2 * height, lanes)
            out_ref[:, at : at + lanes] = both


def term_of(core, first, count, packed_ref, metric_ref):
    width = metric_ref.shape[0]
    orbitals = packed_ref.shape[1] // width
    mine = packed_ref[first : first + count, :].astype(F32)
    mine = mine.reshape(count // 16, 2, 8, orbitals * width)
    mine = jnp.where(core == 0, mine[:, 0], mine[:, 1]).reshape(count // 2, orbitals * width)
    mine = mine.astype(BF16)
    fits = [
        lax.dot_general(
            mine[:, i * width : (i + 1) * width], metric_ref[...], NT, preferred_element_type=F32
        ).astype(BF16)
        for i in range(orbitals)
    ]
    fit = jnp.concatenate(fits, axis=1)
    return lax.dot_general(fit, packed_ref[...], NT, preferred_element_type=F32)


def partner_kernel(core_ref, coef_ref, metric_ref, packed_ref, *out_refs):
    pack(coef_ref, packed_ref)
    term = term_of(1 - core_ref[0], 0, packed_ref.shape[0], packed_ref, metric_ref)
    rows = out_refs[0].shape[0]
    for k, out_ref in enumerate(out_refs):
        out_ref[...] = term[k * rows : (k + 1) * rows]


def own_kernel(core_ref, packed_ref, metric_ref, out_ref):
    out_ref[...] = term_of(core_ref[0], 0, packed_ref.shape[0], packed_ref, metric_ref)


def term_call(kernel, name, out_shape, core, coef, metric):
    width = metric.shape[0]
    columns = coef.size // (2 * width)
    flops = 2 * columns * width * (width + columns)
    return pl.pallas_call(
        kernel,
        out_shape=out_shape,
        in_specs=[SMEM, VMEM, VMEM],
        out_specs=jax.tree.map(lambda _: VMEM, out_shape),
        compiler_params=params(20),
        cost_estimate=pl.CostEstimate(flops=flops, bytes_accessed=6 << 20, transcendentals=0),
        name=name,
    )(core, coef, metric)


def code_kernel(core_ref, sum_ref, *refs):
    *part_refs, out_ref, held, sems = refs
    copies = [
        pltpu.make_async_copy(ref, held.at[k], sems.at[k]) for k, ref in enumerate(part_refs)
    ]
    for copy in copies:
        copy.start()
    core = core_ref[0]
    blocks, rows, columns = out_ref.shape
    lanes = 128
    group = lanes // (2 * rows)
    shape = (group, rows, lanes)
    block = lax.broadcasted_iota(jnp.int32, shape, 0)
    row = lax.broadcasted_iota(jnp.int32, shape, 1)
    column = lax.broadcasted_iota(jnp.int32, shape, 2) - rows * (2 * block + core)
    first = (column == 0) & (row > 0)
    second = (column == 1) & (row == rows - 1)
    groups = blocks // group
    for g in range(groups):
        k, at = divmod(g, groups // len(copies))
        if at == 0:
            copies[k].wait()
        term = sum_ref[g * group * rows : (g + 1) * group * rows, :]
        term += held[k, at * group * rows : (at + 1) * group * rows, :]
        term = term.reshape(group, rows, columns)
        largest = jnp.max(jnp.abs(term), axis=2, keepdims=True)
        code = jnp.ceil(jnp.log2(jnp.maximum(largest, 1e-33)) * 256.0)
        scaled = term * (jnp.exp2(code * (-1.0 / 256.0)) * TOP)
        part = scaled[:, :, g * lanes : (g + 1) * lanes]
        part = jnp.where(first, code, jnp.where(second, code[:, 0:1], part))
        scaled = [scaled[:, :, : g * lanes], part, scaled[:, :, (g + 1) * lanes :]]
        scaled = jnp.concatenate([piece for piece in scaled if piece.size], axis=2)
        out_ref[g * group : (g + 1) * group] = jnp.round(scaled).astype(jnp.int32).astype(jnp.int16)


def code_of(core, total, parts, blocks):
    rows, columns = total.shape
    count = len(parts)
    return pl.pallas_call(
        code_kernel,
        out_shape=jax.ShapeDtypeStruct((blocks, rows // blocks, columns), jnp.int16),
        in_specs=[SMEM, VMEM] + [pl.BlockSpec(memory_space=pl.ANY)] * count,
        out_specs=VMEM,
        scratch_shapes=[
            pltpu.VMEM((count, *parts[0].shape), F32),
            pltpu.SemaphoreType.DMA((count,)),
        ],
        compiler_params=params(16),
        cost_estimate=pl.CostEstimate(flops=0, bytes_accessed=6 << 20, transcendentals=0),
        name="code",
    )(core, total, *parts)


def finish_kernel(me_ref, got_ref, out_ref):
    blocks, rows, columns = got_ref.shape
    lanes = 128
    start = rows * me_ref[0]
    base = pl.multiple_of(start // lanes * lanes, lanes)
    at = start - base
    window = got_ref[:, :, pl.ds(base, lanes)].astype(jnp.int32).astype(F32)
    lane = lax.broadcasted_iota(jnp.int32, window.shape, 2)
    row = lax.broadcasted_iota(jnp.int32, window.shape, 1)
    code = jnp.sum(jnp.where(lane == at, window, 0.0), axis=2, keepdims=True)
    other = jnp.sum(jnp.where(lane == at + 1, window, 0.0), axis=2, keepdims=True)
    code = jnp.where(row[:, :, :1] == 0, other[:, rows - 1 :], code)
    factor = jnp.exp2(code * (1.0 / 256.0)) * (-1.0 / TOP)
    total = jnp.zeros((rows, columns), F32)
    for s in range(blocks):
        total += got_ref[s].astype(jnp.int32).astype(F32) * factor[s]
    out_ref[...] = total
    part = out_ref[:, pl.ds(base, lanes)]
    lane = lax.broadcasted_iota(jnp.int32, part.shape, 1) - at
    row = lax.broadcasted_iota(jnp.int32, part.shape, 0)
    first = jnp.broadcast_to(part[0:1], part.shape)
    mirrored = jnp.sum(jnp.where(lane == row, first, 0.0), axis=1, keepdims=True)
    corner = jnp.sum(jnp.where((lane == rows - 1) & (row == 1), part, 0.0))
    part = jnp.where((lane == 0) & (row > 0), mirrored, part)
    out_ref[:, pl.ds(base, lanes)] = jnp.where((lane == 1) & (row == rows - 1), corner, part)


def finish(me, got):
    return pl.pallas_call(
        finish_kernel,
        out_shape=jax.ShapeDtypeStruct(got.shape[1:], F32),
        in_specs=[SMEM, VMEM],
        out_specs=VMEM,
        compiler_params=params(8),
        name="finish",
    )(me, got)


def body(tensor3, pattern, orbitals, metric):
    ri_local, mu_local, basis = tensor3.shape
    n_wide, n_narrow = lax.axis_size("wide"), lax.axis_size("narrow")
    devices = n_wide * n_narrow
    me = (lax.axis_index("wide") * n_narrow + lax.axis_index("narrow")).astype(jnp.int32)
    core = (lax.axis_index("narrow") & 1).astype(jnp.int32).reshape(1)
    me, core, orbitals = lax.optimization_barrier((me.reshape(1), core, orbitals))
    swap = [(i, i ^ 1) for i in range(n_narrow)]
    orbs = lax.all_to_all(copies_of(orbitals, n_narrow), "narrow", 0, 0, tiled=True)
    orbs = orbs.reshape(basis, orbitals.shape[1])
    parts = coeffs_of(pattern.reshape(-1), orbs, tensor3, devices)
    coef = lax.all_to_all(parts, BOTH, 0, 0, tiled=True)
    coef = coef.reshape(n_wide, n_narrow, 2, mu_local // 2, 2 * ri_local)
    mu = n_narrow * mu_local
    packed = jax.ShapeDtypeStruct((mu, 2 * metric.shape[0]), BF16)
    part = jax.ShapeDtypeStruct((mu // 4, mu), F32)
    packed, *parts = term_call(partner_kernel, "partner", (packed, part, part), core, coef, metric)
    parts = [lax.ppermute(part, "narrow", swap) for part in parts]
    total = jax.ShapeDtypeStruct((mu // 2, mu), F32)
    total = term_call(own_kernel, "own", total, core, packed, metric)
    parts = code_of(core, total, parts, devices // 2)
    sides = [[j for j in range(devices) if j % 2 == c] for c in (0, 1)]
    got = lax.all_to_all(parts, BOTH, 0, 0, tiled=True, axis_index_groups=sides)
    return finish(me, got)


def solution(mesh):
    in_specs = (P("wide", "narrow", None), P("wide", "narrow", None), P("narrow", None), P())
    out_specs = P(("wide", "narrow"), None)
    return jax.shard_map(body, mesh=mesh, in_specs=in_specs, out_specs=out_specs, check_vma=False)
```

```python
import functools

import jax
import jax.numpy as jnp
from jax import lax
from jax.experimental import pallas as pl
from jax.experimental.pallas import tpu as pltpu
from jax.sharding import PartitionSpec as P

BLK = 64
BOTH = ("wide", "narrow")
BF16, F32 = jnp.bfloat16, jnp.float32
TOP = 32766.0
VMEM = pl.BlockSpec(memory_space=pltpu.VMEM)
SMEM = pl.BlockSpec(memory_space=pltpu.SMEM)
NT = (((1,), (1,)), ((), ()))


def params(mib):
    return pltpu.CompilerParams(vmem_limit_bytes=mib << 20)


def copies_kernel(orbitals_ref, out_ref, sems):
    copies = [
        pltpu.make_async_copy(orbitals_ref, out_ref.at[i], sems.at[i])
        for i in range(out_ref.shape[0])
    ]
    for copy in copies:
        copy.start()
    for copy in copies:
        copy.wait()


def copies_of(orbitals, count):
    return pl.pallas_call(
        copies_kernel,
        out_shape=jax.ShapeDtypeStruct((count, *orbitals.shape), BF16),
        in_specs=[pl.BlockSpec(memory_space=pl.ANY)],
        out_specs=pl.BlockSpec(memory_space=pl.ANY),
        scratch_shapes=[pltpu.SemaphoreType.DMA((count,))],
        compiler_params=params(8),
        cost_estimate=pl.CostEstimate(flops=10**10, bytes_accessed=40 << 20, transcendentals=0),
        name="copies",
    )(pltpu.with_memory_space_constraint(orbitals, pltpu.HBM))


def coeffs_kernel(step, pattern_ref, orbs_ref, tensor_ref, out_ref, masked):
    owners, height, lanes = out_ref.shape
    height, ri = height // 2, lanes // 2
    basis, occupied = orbs_ref.shape
    for b in range(basis // BLK):
        rows = pl.ds(b * BLK, BLK)
        masked[rows, :] = (orbs_ref[rows, :].astype(F32) * pattern_ref[b].astype(F32)).astype(BF16)
    for s in range(0, height, step):
        halves = []
        for h in range(2):
            block = tensor_ref[:, h * height + s : h * height + s + step, :]
            value = jnp.dot(
                block.reshape(ri * step, basis), masked[...], preferred_element_type=F32
            )
            value = value.astype(BF16).reshape(ri, step, occupied)
            halves.append(pltpu.einshape("pmi->mpi", value))
        value = jnp.concatenate(halves, axis=1)
        turned = jnp.stack([value[m].T for m in range(step)])
        turned = pltpu.einshape("mjl->jml", turned)
        for i in range(2):
            first = i * height + s
            out_ref[:, first : first + step, :] = turned[i * owners : (i + 1) * owners]


def coeffs_of(pattern, orbs, tensor3, owners, step=8):
    basis, occupied = orbs.shape
    ri, mu, _ = tensor3.shape
    return pl.pallas_call(
        functools.partial(coeffs_kernel, step),
        out_shape=jax.ShapeDtypeStruct((owners, mu, 2 * ri), BF16),
        in_specs=[SMEM, VMEM, VMEM],
        out_specs=VMEM,
        scratch_shapes=[pltpu.VMEM((basis, occupied), BF16)],
        compiler_params=params(20),
        cost_estimate=pl.CostEstimate(
            flops=2 * tensor3.size * occupied, bytes_accessed=2 * tensor3.size, transcendentals=0
        ),
        name="coeffs",
    )(pattern, orbs, tensor3)


def pack(coef_ref, out_ref):
    blocks, wide, orbitals, half, lanes = coef_ref.shape
    height, width = blocks * half, wide * lanes // 2
    low = lax.broadcasted_iota(jnp.int32, (height, lanes), 1) < lanes // 2
    for i in range(orbitals):
        for g in range(wide // 2):
            x = coef_ref[:, 2 * g, i].reshape(height, lanes)
            y = coef_ref[:, 2 * g + 1, i].reshape(height, lanes)
            one = jnp.where(low, x, pltpu.roll(y, lanes // 2, 1)).reshape(blocks, 1, half, lanes)
            two = jnp.where(low, pltpu.roll(x, lanes // 2, 1), y).reshape(blocks, 1, half, lanes)
            at = i * width + g * lanes
            both = jnp.concatenate([one, two], axis=1).reshape(2 * height, lanes)
            out_ref[:, at : at + lanes] = both


def term_of(core, first, count, packed_ref, metric_ref):
    width = metric_ref.shape[0]
    orbitals = packed_ref.shape[1] // width
    mine = packed_ref[first : first + count, :].astype(F32)
    mine = mine.reshape(count // 16, 2, 8, orbitals * width)
    mine = jnp.where(core == 0, mine[:, 0], mine[:, 1]).reshape(count // 2, orbitals * width)
    mine = mine.astype(BF16)
    fits = [
        lax.dot_general(
            mine[:, i * width : (i + 1) * width], metric_ref[...], NT, preferred_element_type=F32
        ).astype(BF16)
        for i in range(orbitals)
    ]
    fit = jnp.concatenate(fits, axis=1)
    return lax.dot_general(fit, packed_ref[...], NT, preferred_element_type=F32)


def partner_kernel(core_ref, coef_ref, metric_ref, packed_ref, *out_refs):
    pack(coef_ref, packed_ref)
    term = term_of(1 - core_ref[0], 0, packed_ref.shape[0], packed_ref, metric_ref)
    rows = out_refs[0].shape[0]
    for k, out_ref in enumerate(out_refs):
        out_ref[...] = term[k * rows : (k + 1) * rows]


def own_kernel(core_ref, packed_ref, metric_ref, out_ref):
    out_ref[...] = term_of(core_ref[0], 0, packed_ref.shape[0], packed_ref, metric_ref)


def term_call(kernel, name, out_shape, core, coef, metric):
    width = metric.shape[0]
    columns = coef.size // (2 * width)
    flops = 2 * columns * width * (width + columns)
    return pl.pallas_call(
        kernel,
        out_shape=out_shape,
        in_specs=[SMEM, VMEM, VMEM],
        out_specs=jax.tree.map(lambda _: VMEM, out_shape),
        compiler_params=params(20),
        cost_estimate=pl.CostEstimate(flops=flops, bytes_accessed=6 << 20, transcendentals=0),
        name=name,
    )(core, coef, metric)


def code_kernel(core_ref, sum_ref, *refs):
    *part_refs, out_ref, held, sems = refs
    copies = [
        pltpu.make_async_copy(ref, held.at[k], sems.at[k]) for k, ref in enumerate(part_refs)
    ]
    for copy in copies:
        copy.start()
    core = core_ref[0]
    blocks, rows, columns = out_ref.shape
    lanes = 128
    group = lanes // (2 * rows)
    shape = (group, rows, lanes)
    block = lax.broadcasted_iota(jnp.int32, shape, 0)
    row = lax.broadcasted_iota(jnp.int32, shape, 1)
    column = lax.broadcasted_iota(jnp.int32, shape, 2) - rows * (2 * block + core)
    first = (column == 0) & (row > 0)
    second = (column == 1) & (row == rows - 1)
    groups = blocks // group
    for g in range(groups):
        k, at = divmod(g, groups // len(copies))
        if at == 0:
            copies[k].wait()
        term = sum_ref[g * group * rows : (g + 1) * group * rows, :]
        term += held[k, at * group * rows : (at + 1) * group * rows, :]
        term = term.reshape(group, rows, columns)
        largest = jnp.max(jnp.abs(term), axis=2, keepdims=True)
        code = jnp.ceil(jnp.log2(jnp.maximum(largest, 1e-33)) * 256.0)
        scaled = term * (jnp.exp2(code * (-1.0 / 256.0)) * TOP)
        part = scaled[:, :, g * lanes : (g + 1) * lanes]
        part = jnp.where(first, code, jnp.where(second, code[:, 0:1], part))
        scaled = [scaled[:, :, : g * lanes], part, scaled[:, :, (g + 1) * lanes :]]
        scaled = jnp.concatenate([piece for piece in scaled if piece.size], axis=2)
        out_ref[g * group : (g + 1) * group] = jnp.round(scaled).astype(jnp.int32).astype(jnp.int16)


def code_of(core, total, parts, blocks):
    rows, columns = total.shape
    count = len(parts)
    return pl.pallas_call(
        code_kernel,
        out_shape=jax.ShapeDtypeStruct((blocks, rows // blocks, columns), jnp.int16),
        in_specs=[SMEM, VMEM] + [pl.BlockSpec(memory_space=pl.ANY)] * count,
        out_specs=VMEM,
        scratch_shapes=[
            pltpu.VMEM((count, *parts[0].shape), F32),
            pltpu.SemaphoreType.DMA((count,)),
        ],
        compiler_params=params(16),
        cost_estimate=pl.CostEstimate(flops=0, bytes_accessed=6 << 20, transcendentals=0),
        name="code",
    )(core, total, *parts)


def finish_kernel(me_ref, got_ref, out_ref):
    blocks, rows, columns = got_ref.shape
    lanes = 128
    start = rows * me_ref[0]
    base = pl.multiple_of(start // lanes * lanes, lanes)
    at = start - base
    window = got_ref[:, :, pl.ds(base, lanes)].astype(jnp.int32).astype(F32)
    lane = lax.broadcasted_iota(jnp.int32, window.shape, 2)
    row = lax.broadcasted_iota(jnp.int32, window.shape, 1)
    code = jnp.sum(jnp.where(lane == at, window, 0.0), axis=2, keepdims=True)
    other = jnp.sum(jnp.where(lane == at + 1, window, 0.0), axis=2, keepdims=True)
    code = jnp.where(row[:, :, :1] == 0, other[:, rows - 1 :], code)
    factor = jnp.exp2(code * (1.0 / 256.0)) * (-1.0 / TOP)
    total = jnp.zeros((rows, columns), F32)
    for s in range(blocks):
        total += got_ref[s].astype(jnp.int32).astype(F32) * factor[s]
    out_ref[...] = total
    part = out_ref[:, pl.ds(base, lanes)]
    lane = lax.broadcasted_iota(jnp.int32, part.shape, 1) - at
    row = lax.broadcasted_iota(jnp.int32, part.shape, 0)
    first = jnp.broadcast_to(part[0:1], part.shape)
    mirrored = jnp.sum(jnp.where(lane == row, first, 0.0), axis=1, keepdims=True)
    corner = jnp.sum(jnp.where((lane == rows - 1) & (row == 1), part, 0.0))
    part = jnp.where((lane == 0) & (row > 0), mirrored, part)
    out_ref[:, pl.ds(base, lanes)] = jnp.where((lane == 1) & (row == rows - 1), corner, part)


def finish(me, got):
    return pl.pallas_call(
        finish_kernel,
        out_shape=jax.ShapeDtypeStruct(got.shape[1:], F32),
        in_specs=[SMEM, VMEM],
        out_specs=VMEM,
        compiler_params=params(8),
        name="finish",
    )(me, got)


def body(tensor3, pattern, orbitals, metric):
    ri_local, mu_local, basis = tensor3.shape
    n_wide, n_narrow = lax.axis_size("wide"), lax.axis_size("narrow")
    devices = n_wide * n_narrow
    me = (lax.axis_index("wide") * n_narrow + lax.axis_index("narrow")).astype(jnp.int32)
    core = (lax.axis_index("narrow") & 1).astype(jnp.int32).reshape(1)
    me, core, orbitals = lax.optimization_barrier((me.reshape(1), core, orbitals))
    swap = [(i, i ^ 1) for i in range(n_narrow)]
    orbs = lax.all_to_all(copies_of(orbitals, n_narrow), "narrow", 0, 0, tiled=True)
    orbs = orbs.reshape(basis, orbitals.shape[1])
    parts = coeffs_of(pattern.reshape(-1), orbs, tensor3, devices)
    coef = lax.all_to_all(parts, ("narrow", "wide"), 0, 0, tiled=True)
    coef = coef.reshape(n_narrow, n_wide, 2, mu_local // 2, 2 * ri_local)
    mu = n_narrow * mu_local
    packed = jax.ShapeDtypeStruct((mu, 2 * metric.shape[0]), BF16)
    part = jax.ShapeDtypeStruct((mu // 4, mu), F32)
    packed, *parts = term_call(partner_kernel, "partner", (packed, part, part), core, coef, metric)
    parts = [lax.ppermute(part, "narrow", swap) for part in parts]
    total = jax.ShapeDtypeStruct((mu // 2, mu), F32)
    total = term_call(own_kernel, "own", total, core, packed, metric)
    parts = code_of(core, total, parts, devices // 2)
    sides = [[j for j in range(devices) if j % 2 == c] for c in (0, 1)]
    got = lax.all_to_all(parts, BOTH, 0, 0, tiled=True, axis_index_groups=sides)
    return finish(me, got)


def solution(mesh):
    in_specs = (P("wide", "narrow", None), P("wide", "narrow", None), P("narrow", None), P())
    out_specs = P(("wide", "narrow"), None)
    return jax.shard_map(body, mesh=mesh, in_specs=in_specs, out_specs=out_specs, check_vma=False)
```

```python
import functools

import jax
import jax.numpy as jnp
from jax import lax
from jax.experimental import pallas as pl
from jax.experimental.pallas import tpu as pltpu
from jax.sharding import PartitionSpec as P

BLK = 64
BOTH = ("wide", "narrow")
BF16, F32 = jnp.bfloat16, jnp.float32
TOP = 32766.0
VMEM = pl.BlockSpec(memory_space=pltpu.VMEM)
SMEM = pl.BlockSpec(memory_space=pltpu.SMEM)
NT = (((1,), (1,)), ((), ()))


def params(mib):
    return pltpu.CompilerParams(vmem_limit_bytes=mib << 20)


def copies_kernel(orbitals_ref, out_ref, sems):
    copies = [
        pltpu.make_async_copy(orbitals_ref, out_ref.at[i], sems.at[i])
        for i in range(out_ref.shape[0])
    ]
    for copy in copies:
        copy.start()
    for copy in copies:
        copy.wait()


def copies_of(orbitals, count):
    return pl.pallas_call(
        copies_kernel,
        out_shape=jax.ShapeDtypeStruct((count, *orbitals.shape), BF16),
        in_specs=[pl.BlockSpec(memory_space=pl.ANY)],
        out_specs=pl.BlockSpec(memory_space=pl.ANY),
        scratch_shapes=[pltpu.SemaphoreType.DMA((count,))],
        compiler_params=params(8),
        cost_estimate=pl.CostEstimate(flops=10**10, bytes_accessed=40 << 20, transcendentals=0),
        name="copies",
    )(pltpu.with_memory_space_constraint(orbitals, pltpu.HBM))


def coeffs_kernel(step, core_ref, pattern_ref, mine_ref, other_ref, tensor_ref, out_ref, masked):
    owners, height, lanes = out_ref.shape
    height, ri = height // 2, lanes // 2
    basis, occupied = masked.shape
    for b in range(mine_ref.shape[0]):
        for orbs_ref, core in ((mine_ref, core_ref[0]), (other_ref, 1 - core_ref[0])):
            rows = pl.ds(pl.multiple_of((2 * b + core) * BLK, BLK), BLK)
            keep = pattern_ref[2 * b + core].astype(F32)
            masked[rows, :] = (orbs_ref[b].astype(F32) * keep).astype(BF16)
    for s in range(0, height, step):
        halves = []
        for h in range(2):
            block = tensor_ref[:, h * height + s : h * height + s + step, :]
            value = jnp.dot(
                block.reshape(ri * step, basis), masked[...], preferred_element_type=F32
            )
            value = value.astype(BF16).reshape(ri, step, occupied)
            halves.append(pltpu.einshape("pmi->mpi", value))
        value = jnp.concatenate(halves, axis=1)
        turned = jnp.stack([value[m].T for m in range(step)])
        turned = pltpu.einshape("mjl->jml", turned)
        for i in range(2):
            first = i * height + s
            out_ref[:, first : first + step, :] = turned[i * owners : (i + 1) * owners]


def coeffs_of(core, pattern, mine, other, tensor3, owners, step=8):
    occupied = mine.shape[2]
    ri, mu, basis = tensor3.shape
    return pl.pallas_call(
        functools.partial(coeffs_kernel, step),
        out_shape=jax.ShapeDtypeStruct((owners, mu, 2 * ri), BF16),
        in_specs=[SMEM, SMEM, VMEM, VMEM, VMEM],
        out_specs=VMEM,
        scratch_shapes=[pltpu.VMEM((basis, occupied), BF16)],
        compiler_params=params(20),
        cost_estimate=pl.CostEstimate(
            flops=2 * tensor3.size * occupied, bytes_accessed=2 * tensor3.size, transcendentals=0
        ),
        name="coeffs",
    )(core, pattern, mine, other, tensor3)


def pack(coef_ref, out_ref):
    wide, blocks, orbitals, half, lanes = coef_ref.shape
    height, width = blocks * half, wide * lanes // 2
    low = lax.broadcasted_iota(jnp.int32, (height, lanes), 1) < lanes // 2
    for i in range(orbitals):
        for g in range(wide // 2):
            x = coef_ref[2 * g, :, i].reshape(height, lanes)
            y = coef_ref[2 * g + 1, :, i].reshape(height, lanes)
            one = jnp.where(low, x, pltpu.roll(y, lanes // 2, 1)).reshape(blocks, 1, half, lanes)
            two = jnp.where(low, pltpu.roll(x, lanes // 2, 1), y).reshape(blocks, 1, half, lanes)
            at = i * width + g * lanes
            both = jnp.concatenate([one, two], axis=1).reshape(2 * height, lanes)
            out_ref[:, at : at + lanes] = both


def term_of(core, first, count, packed_ref, metric_ref):
    width = metric_ref.shape[0]
    orbitals = packed_ref.shape[1] // width
    mine = packed_ref[first : first + count, :].astype(F32)
    mine = mine.reshape(count // 16, 2, 8, orbitals * width)
    mine = jnp.where(core == 0, mine[:, 0], mine[:, 1]).reshape(count // 2, orbitals * width)
    mine = mine.astype(BF16)
    fits = [
        lax.dot_general(
            mine[:, i * width : (i + 1) * width], metric_ref[...], NT, preferred_element_type=F32
        ).astype(BF16)
        for i in range(orbitals)
    ]
    fit = jnp.concatenate(fits, axis=1)
    return lax.dot_general(fit, packed_ref[...], NT, preferred_element_type=F32)


def partner_kernel(core_ref, coef_ref, metric_ref, packed_ref, *out_refs):
    pack(coef_ref, packed_ref)
    term = term_of(1 - core_ref[0], 0, packed_ref.shape[0], packed_ref, metric_ref)
    rows = out_refs[0].shape[0]
    for k, out_ref in enumerate(out_refs):
        out_ref[...] = term[k * rows : (k + 1) * rows]


def own_kernel(core_ref, packed_ref, metric_ref, out_ref):
    out_ref[...] = term_of(core_ref[0], 0, packed_ref.shape[0], packed_ref, metric_ref)


def term_call(kernel, name, out_shape, core, coef, metric):
    width = metric.shape[0]
    columns = coef.size // (2 * width)
    flops = 2 * columns * width * (width + columns)
    return pl.pallas_call(
        kernel,
        out_shape=out_shape,
        in_specs=[SMEM, VMEM, VMEM],
        out_specs=jax.tree.map(lambda _: VMEM, out_shape),
        compiler_params=params(20),
        cost_estimate=pl.CostEstimate(flops=flops, bytes_accessed=6 << 20, transcendentals=0),
        name=name,
    )(core, coef, metric)


def code_kernel(core_ref, sum_ref, *refs):
    *part_refs, out_ref, held, sems = refs
    copies = [
        pltpu.make_async_copy(ref, held.at[k], sems.at[k]) for k, ref in enumerate(part_refs)
    ]
    for copy in copies:
        copy.start()
    core = core_ref[0]
    blocks, rows, columns = out_ref.shape
    lanes = 128
    group = lanes // (2 * rows)
    shape = (group, rows, lanes)
    block = lax.broadcasted_iota(jnp.int32, shape, 0)
    row = lax.broadcasted_iota(jnp.int32, shape, 1)
    column = lax.broadcasted_iota(jnp.int32, shape, 2) - rows * (2 * block + core)
    first = (column == 0) & (row > 0)
    second = (column == 1) & (row == rows - 1)
    groups = blocks // group
    for g in range(groups):
        k, at = divmod(g, groups // len(copies))
        if at == 0:
            copies[k].wait()
        term = sum_ref[g * group * rows : (g + 1) * group * rows, :]
        term += held[k, at * group * rows : (at + 1) * group * rows, :]
        term = term.reshape(group, rows, columns)
        largest = jnp.max(jnp.abs(term), axis=2, keepdims=True)
        code = jnp.ceil(jnp.log2(jnp.maximum(largest, 1e-33)) * 256.0)
        scaled = term * (jnp.exp2(code * (-1.0 / 256.0)) * TOP)
        part = scaled[:, :, g * lanes : (g + 1) * lanes]
        part = jnp.where(first, code, jnp.where(second, code[:, 0:1], part))
        scaled = [scaled[:, :, : g * lanes], part, scaled[:, :, (g + 1) * lanes :]]
        scaled = jnp.concatenate([piece for piece in scaled if piece.size], axis=2)
        out_ref[g * group : (g + 1) * group] = jnp.round(scaled).astype(jnp.int32).astype(jnp.int16)


def code_of(core, total, parts, blocks):
    rows, columns = total.shape
    count = len(parts)
    return pl.pallas_call(
        code_kernel,
        out_shape=jax.ShapeDtypeStruct((blocks, rows // blocks, columns), jnp.int16),
        in_specs=[SMEM, VMEM] + [pl.BlockSpec(memory_space=pl.ANY)] * count,
        out_specs=VMEM,
        scratch_shapes=[
            pltpu.VMEM((count, *parts[0].shape), F32),
            pltpu.SemaphoreType.DMA((count,)),
        ],
        compiler_params=params(16),
        cost_estimate=pl.CostEstimate(flops=0, bytes_accessed=6 << 20, transcendentals=0),
        name="code",
    )(core, total, *parts)


def finish_kernel(me_ref, got_ref, out_ref):
    blocks, rows, columns = got_ref.shape
    lanes = 128
    start = rows * me_ref[0]
    base = pl.multiple_of(start // lanes * lanes, lanes)
    at = start - base
    window = got_ref[:, :, pl.ds(base, lanes)].astype(jnp.int32).astype(F32)
    lane = lax.broadcasted_iota(jnp.int32, window.shape, 2)
    row = lax.broadcasted_iota(jnp.int32, window.shape, 1)
    code = jnp.sum(jnp.where(lane == at, window, 0.0), axis=2, keepdims=True)
    other = jnp.sum(jnp.where(lane == at + 1, window, 0.0), axis=2, keepdims=True)
    code = jnp.where(row[:, :, :1] == 0, other[:, rows - 1 :], code)
    factor = jnp.exp2(code * (1.0 / 256.0)) * (-1.0 / TOP)
    total = jnp.zeros((rows, columns), F32)
    for s in range(blocks):
        total += got_ref[s].astype(jnp.int32).astype(F32) * factor[s]
    out_ref[...] = total
    part = out_ref[:, pl.ds(base, lanes)]
    lane = lax.broadcasted_iota(jnp.int32, part.shape, 1) - at
    row = lax.broadcasted_iota(jnp.int32, part.shape, 0)
    first = jnp.broadcast_to(part[0:1], part.shape)
    mirrored = jnp.sum(jnp.where(lane == row, first, 0.0), axis=1, keepdims=True)
    corner = jnp.sum(jnp.where((lane == rows - 1) & (row == 1), part, 0.0))
    part = jnp.where((lane == 0) & (row > 0), mirrored, part)
    out_ref[:, pl.ds(base, lanes)] = jnp.where((lane == 1) & (row == rows - 1), corner, part)


def finish(me, got):
    return pl.pallas_call(
        finish_kernel,
        out_shape=jax.ShapeDtypeStruct(got.shape[1:], F32),
        in_specs=[SMEM, VMEM],
        out_specs=VMEM,
        compiler_params=params(8),
        name="finish",
    )(me, got)


def body(tensor3, pattern, orbitals, metric):
    ri_local, mu_local, basis = tensor3.shape
    n_wide, n_narrow = lax.axis_size("wide"), lax.axis_size("narrow")
    devices = n_wide * n_narrow
    me = (lax.axis_index("wide") * n_narrow + lax.axis_index("narrow")).astype(jnp.int32)
    core = (lax.axis_index("narrow") & 1).astype(jnp.int32).reshape(1)
    me, core, orbitals = lax.optimization_barrier((me.reshape(1), core, orbitals))
    swap = [(i, i ^ 1) for i in range(n_narrow)]
    sides = [[i for i in range(n_narrow) if i % 2 == c] for c in (0, 1)]
    copies = copies_of(orbitals, n_narrow // 2)
    mine = lax.all_to_all(copies, "narrow", 0, 0, tiled=True, axis_index_groups=sides)
    other = lax.ppermute(mine, "narrow", swap)
    parts = coeffs_of(core, pattern.reshape(-1), mine, other, tensor3, devices)
    coef = lax.all_to_all(parts, BOTH, 0, 0, tiled=True)
    coef = coef.reshape(n_wide, n_narrow, 2, mu_local // 2, 2 * ri_local)
    mu = n_narrow * mu_local
    packed = jax.ShapeDtypeStruct((mu, 2 * metric.shape[0]), BF16)
    part = jax.ShapeDtypeStruct((mu // 4, mu), F32)
    packed, *parts = term_call(partner_kernel, "partner", (packed, part, part), core, coef, metric)
    parts = [lax.ppermute(part, "narrow", swap) for part in parts]
    total = jax.ShapeDtypeStruct((mu // 2, mu), F32)
    total = term_call(own_kernel, "own", total, core, packed, metric)
    parts = code_of(core, total, parts, devices // 2)
    sides = [[j for j in range(devices) if j % 2 == c] for c in (0, 1)]
    got = lax.all_to_all(parts, BOTH, 0, 0, tiled=True, axis_index_groups=sides)
    return finish(me, got)


def solution(mesh):
    in_specs = (P("wide", "narrow", None), P("wide", "narrow", None), P("narrow", None), P())
    out_specs = P(("wide", "narrow"), None)
    return jax.shard_map(body, mesh=mesh, in_specs=in_specs, out_specs=out_specs, check_vma=False)
```

```python
import functools

import jax
import jax.numpy as jnp
from jax import lax
from jax.experimental import pallas as pl
from jax.experimental.pallas import tpu as pltpu
from jax.sharding import PartitionSpec as P

BLK = 64
BOTH = ("wide", "narrow")
BF16, F32 = jnp.bfloat16, jnp.float32
TOP = 32766.0
VMEM = pl.BlockSpec(memory_space=pltpu.VMEM)
SMEM = pl.BlockSpec(memory_space=pltpu.SMEM)
NT = (((1,), (1,)), ((), ()))


def params(mib):
    return pltpu.CompilerParams(vmem_limit_bytes=mib << 20)


def copies_kernel(orbitals_ref, out_ref, sems):
    copies = [
        pltpu.make_async_copy(orbitals_ref, out_ref.at[i], sems.at[i])
        for i in range(out_ref.shape[0])
    ]
    for copy in copies:
        copy.start()
    for copy in copies:
        copy.wait()


def copies_of(orbitals, count):
    return pl.pallas_call(
        copies_kernel,
        out_shape=jax.ShapeDtypeStruct((count, *orbitals.shape), BF16),
        in_specs=[pl.BlockSpec(memory_space=pl.ANY)],
        out_specs=pl.BlockSpec(memory_space=pl.ANY),
        scratch_shapes=[pltpu.SemaphoreType.DMA((count,))],
        compiler_params=params(8),
        cost_estimate=pl.CostEstimate(flops=10**10, bytes_accessed=40 << 20, transcendentals=0),
        name="copies",
    )(pltpu.with_memory_space_constraint(orbitals, pltpu.HBM))


def coeffs_kernel(step, core_ref, pattern_ref, mine_ref, other_ref, tensor_ref, out_ref, masked):
    owners, height, lanes = out_ref.shape
    height, ri = height // 2, lanes // 2
    basis, occupied = masked.shape
    for b in range(mine_ref.shape[0]):
        for orbs_ref, core in ((mine_ref, core_ref[0]), (other_ref, 1 - core_ref[0])):
            rows = pl.ds(pl.multiple_of((2 * b + core) * BLK, BLK), BLK)
            keep = pattern_ref[2 * b + core].astype(F32)
            masked[rows, :] = (orbs_ref[b].astype(F32) * keep).astype(BF16)
    for s in range(0, height, step):
        halves = []
        for h in range(2):
            block = tensor_ref[:, h * height + s : h * height + s + step, :]
            value = jnp.dot(
                block.reshape(ri * step, basis), masked[...], preferred_element_type=F32
            )
            value = value.astype(BF16).reshape(ri, step, occupied)
            halves.append(pltpu.einshape("pmi->mpi", value))
        value = jnp.concatenate(halves, axis=1)
        turned = jnp.stack([value[m].T for m in range(step)])
        turned = pltpu.einshape("mjl->jml", turned)
        for i in range(2):
            first = i * height + s
            out_ref[:, first : first + step, :] = turned[i * owners : (i + 1) * owners]


def coeffs_of(core, pattern, mine, other, tensor3, owners, step=8):
    occupied = mine.shape[2]
    ri, mu, basis = tensor3.shape
    return pl.pallas_call(
        functools.partial(coeffs_kernel, step),
        out_shape=jax.ShapeDtypeStruct((owners, mu, 2 * ri), BF16),
        in_specs=[SMEM, SMEM, VMEM, VMEM, VMEM],
        out_specs=VMEM,
        scratch_shapes=[pltpu.VMEM((basis, occupied), BF16)],
        compiler_params=params(20),
        cost_estimate=pl.CostEstimate(
            flops=2 * tensor3.size * occupied, bytes_accessed=2 * tensor3.size, transcendentals=0
        ),
        name="coeffs",
    )(core, pattern, mine, other, tensor3)


def pack(coef_ref, out_ref):
    wide, blocks, orbitals, half, lanes = coef_ref.shape
    height, width = blocks * half, wide * lanes // 2
    low = lax.broadcasted_iota(jnp.int32, (height, lanes), 1) < lanes // 2
    for i in range(orbitals):
        for g in range(wide // 2):
            x = coef_ref[2 * g, :, i].reshape(height, lanes)
            y = coef_ref[2 * g + 1, :, i].reshape(height, lanes)
            one = jnp.where(low, x, pltpu.roll(y, lanes // 2, 1)).reshape(blocks, 1, half, lanes)
            two = jnp.where(low, pltpu.roll(x, lanes // 2, 1), y).reshape(blocks, 1, half, lanes)
            at = i * width + g * lanes
            both = jnp.concatenate([one, two], axis=1).reshape(2 * height, lanes)
            out_ref[:, at : at + lanes] = both


def coded(term, axis):
    largest = jnp.max(jnp.abs(term), axis=axis, keepdims=True)
    code = jnp.ceil(jnp.log2(jnp.maximum(largest, 1e-33)) * 256.0)
    return code, term * (jnp.exp2(code * (-1.0 / 256.0)) * TOP)


def term_of(core, first, count, packed_ref, metric_ref):
    width = metric_ref.shape[0]
    orbitals = packed_ref.shape[1] // width
    mine = packed_ref[first : first + count, :].astype(F32)
    mine = mine.reshape(count // 16, 2, 8, orbitals * width)
    mine = jnp.where(core == 0, mine[:, 0], mine[:, 1]).reshape(count // 2, orbitals * width)
    mine = mine.astype(BF16)
    fits = [
        lax.dot_general(
            mine[:, i * width : (i + 1) * width], metric_ref[...], NT, preferred_element_type=F32
        ).astype(BF16)
        for i in range(orbitals)
    ]
    fit = jnp.concatenate(fits, axis=1)
    return lax.dot_general(fit, packed_ref[...], NT, preferred_element_type=F32)


def partner_kernel(core_ref, coef_ref, metric_ref, packed_ref, out_ref):
    pack(coef_ref, packed_ref)
    term = term_of(1 - core_ref[0], 0, packed_ref.shape[0], packed_ref, metric_ref)
    columns = term.shape[1]
    code, scaled = coded(term, 1)
    out_ref[:, :columns] = jnp.round(scaled).astype(jnp.int32).astype(jnp.int16)
    tail = (term.shape[0], out_ref.shape[1] - columns)
    out_ref[:, columns:] = jnp.broadcast_to(code.astype(jnp.int32), tail).astype(jnp.int16)


def own_kernel(core_ref, packed_ref, metric_ref, out_ref):
    out_ref[...] = term_of(core_ref[0], 0, packed_ref.shape[0], packed_ref, metric_ref)


def term_call(kernel, name, out_shape, core, coef, metric):
    width = metric.shape[0]
    columns = coef.size // (2 * width)
    flops = 2 * columns * width * (width + columns)
    return pl.pallas_call(
        kernel,
        out_shape=out_shape,
        in_specs=[SMEM, VMEM, VMEM],
        out_specs=jax.tree.map(lambda _: VMEM, out_shape),
        compiler_params=params(20),
        cost_estimate=pl.CostEstimate(flops=flops, bytes_accessed=6 << 20, transcendentals=0),
        name=name,
    )(core, coef, metric)


def code_kernel(core_ref, sum_ref, other_ref, out_ref, held, sem):
    copy = pltpu.make_async_copy(other_ref, held, sem)
    copy.start()
    core = core_ref[0]
    blocks, rows, columns = out_ref.shape
    lanes = 128
    group = lanes // (2 * rows)
    shape = (group, rows, lanes)
    block = lax.broadcasted_iota(jnp.int32, shape, 0)
    row = lax.broadcasted_iota(jnp.int32, shape, 1)
    column = lax.broadcasted_iota(jnp.int32, shape, 2) - rows * (2 * block + core)
    first = (column == 0) & (row > 0)
    second = (column == 1) & (row == rows - 1)
    copy.wait()
    for g in range(blocks // group):
        some = slice(g * group * rows, (g + 1) * group * rows)
        other = held[some, :columns].astype(jnp.int32).astype(F32)
        power = held[some, columns : columns + 1].astype(jnp.int32).astype(F32)
        term = sum_ref[some, :] + other * (jnp.exp2(power * (1.0 / 256.0)) * (1.0 / TOP))
        term = term.reshape(group, rows, columns)
        code, scaled = coded(term, 2)
        part = scaled[:, :, g * lanes : (g + 1) * lanes]
        part = jnp.where(first, code, jnp.where(second, code[:, 0:1], part))
        scaled = [scaled[:, :, : g * lanes], part, scaled[:, :, (g + 1) * lanes :]]
        scaled = jnp.concatenate([piece for piece in scaled if piece.size], axis=2)
        out_ref[g * group : (g + 1) * group] = jnp.round(scaled).astype(jnp.int32).astype(jnp.int16)


def code_of(core, total, other, blocks):
    rows, columns = total.shape
    return pl.pallas_call(
        code_kernel,
        out_shape=jax.ShapeDtypeStruct((blocks, rows // blocks, columns), jnp.int16),
        in_specs=[SMEM, VMEM, pl.BlockSpec(memory_space=pl.ANY)],
        out_specs=VMEM,
        scratch_shapes=[pltpu.VMEM(other.shape, jnp.int16), pltpu.SemaphoreType.DMA],
        compiler_params=params(16),
        cost_estimate=pl.CostEstimate(flops=0, bytes_accessed=6 << 20, transcendentals=0),
        name="code",
    )(core, total, other)


def finish_kernel(me_ref, got_ref, out_ref):
    blocks, rows, columns = got_ref.shape
    lanes = 128
    start = rows * me_ref[0]
    base = pl.multiple_of(start // lanes * lanes, lanes)
    at = start - base
    window = got_ref[:, :, pl.ds(base, lanes)].astype(jnp.int32).astype(F32)
    lane = lax.broadcasted_iota(jnp.int32, window.shape, 2)
    row = lax.broadcasted_iota(jnp.int32, window.shape, 1)
    code = jnp.sum(jnp.where(lane == at, window, 0.0), axis=2, keepdims=True)
    other = jnp.sum(jnp.where(lane == at + 1, window, 0.0), axis=2, keepdims=True)
    code = jnp.where(row[:, :, :1] == 0, other[:, rows - 1 :], code)
    factor = jnp.exp2(code * (1.0 / 256.0)) * (-1.0 / TOP)
    total = jnp.zeros((rows, columns), F32)
    for s in range(blocks):
        total += got_ref[s].astype(jnp.int32).astype(F32) * factor[s]
    out_ref[...] = total
    part = out_ref[:, pl.ds(base, lanes)]
    lane = lax.broadcasted_iota(jnp.int32, part.shape, 1) - at
    row = lax.broadcasted_iota(jnp.int32, part.shape, 0)
    first = jnp.broadcast_to(part[0:1], part.shape)
    mirrored = jnp.sum(jnp.where(lane == row, first, 0.0), axis=1, keepdims=True)
    corner = jnp.sum(jnp.where((lane == rows - 1) & (row == 1), part, 0.0))
    part = jnp.where((lane == 0) & (row > 0), mirrored, part)
    out_ref[:, pl.ds(base, lanes)] = jnp.where((lane == 1) & (row == rows - 1), corner, part)


def finish(me, got):
    return pl.pallas_call(
        finish_kernel,
        out_shape=jax.ShapeDtypeStruct(got.shape[1:], F32),
        in_specs=[SMEM, VMEM],
        out_specs=VMEM,
        compiler_params=params(8),
        name="finish",
    )(me, got)


def body(tensor3, pattern, orbitals, metric):
    ri_local, mu_local, basis = tensor3.shape
    n_wide, n_narrow = lax.axis_size("wide"), lax.axis_size("narrow")
    devices = n_wide * n_narrow
    me = (lax.axis_index("wide") * n_narrow + lax.axis_index("narrow")).astype(jnp.int32)
    core = (lax.axis_index("narrow") & 1).astype(jnp.int32).reshape(1)
    me, core, orbitals = lax.optimization_barrier((me.reshape(1), core, orbitals))
    swap = [(i, i ^ 1) for i in range(n_narrow)]
    sides = [[i for i in range(n_narrow) if i % 2 == c] for c in (0, 1)]
    copies = copies_of(orbitals, n_narrow // 2)
    mine = lax.all_to_all(copies, "narrow", 0, 0, tiled=True, axis_index_groups=sides)
    other = lax.ppermute(mine, "narrow", swap)
    parts = coeffs_of(core, pattern.reshape(-1), mine, other, tensor3, devices)
    coef = lax.all_to_all(parts, BOTH, 0, 0, tiled=True)
    coef = coef.reshape(n_wide, n_narrow, 2, mu_local // 2, 2 * ri_local)
    mu = n_narrow * mu_local
    packed = jax.ShapeDtypeStruct((mu, 2 * metric.shape[0]), BF16)
    part = jax.ShapeDtypeStruct((mu // 2, mu + 128), jnp.int16)
    packed, other = term_call(partner_kernel, "partner", (packed, part), core, coef, metric)
    other = lax.ppermute(other, "narrow", swap)
    total = jax.ShapeDtypeStruct((mu // 2, mu), F32)
    total = term_call(own_kernel, "own", total, core, packed, metric)
    parts = code_of(core, total, other, devices // 2)
    sides = [[j for j in range(devices) if j % 2 == c] for c in (0, 1)]
    got = lax.all_to_all(parts, BOTH, 0, 0, tiled=True, axis_index_groups=sides)
    return finish(me, got)


def solution(mesh):
    in_specs = (P("wide", "narrow", None), P("wide", "narrow", None), P("narrow", None), P())
    out_specs = P(("wide", "narrow"), None)
    return jax.shard_map(body, mesh=mesh, in_specs=in_specs, out_specs=out_specs, check_vma=False)
```

```python
import functools

import jax
import jax.numpy as jnp
from jax import lax
from jax.experimental import pallas as pl
from jax.experimental.pallas import tpu as pltpu
from jax.sharding import PartitionSpec as P

BLK = 64
BOTH = ("wide", "narrow")
BF16, F32 = jnp.bfloat16, jnp.float32
TOP = 32766.0
VMEM = pl.BlockSpec(memory_space=pltpu.VMEM)
SMEM = pl.BlockSpec(memory_space=pltpu.SMEM)
NT = (((1,), (1,)), ((), ()))


def params(mib):
    return pltpu.CompilerParams(vmem_limit_bytes=mib << 20)


def copies_kernel(orbitals_ref, out_ref, sems):
    copies = [
        pltpu.make_async_copy(orbitals_ref, out_ref.at[i], sems.at[i])
        for i in range(out_ref.shape[0])
    ]
    for copy in copies:
        copy.start()
    for copy in copies:
        copy.wait()


def copies_of(orbitals, count):
    return pl.pallas_call(
        copies_kernel,
        out_shape=jax.ShapeDtypeStruct((count, *orbitals.shape), BF16),
        in_specs=[pl.BlockSpec(memory_space=pl.ANY)],
        out_specs=pl.BlockSpec(memory_space=pl.ANY),
        scratch_shapes=[pltpu.SemaphoreType.DMA((count,))],
        compiler_params=params(8),
        cost_estimate=pl.CostEstimate(flops=10**10, bytes_accessed=40 << 20, transcendentals=0),
        name="copies",
    )(pltpu.with_memory_space_constraint(orbitals, pltpu.HBM))


def coeffs_kernel(step, core_ref, pattern_ref, mine_ref, other_ref, tensor_ref, out_ref, masked):
    owners, height, lanes = out_ref.shape
    height, ri = height // 2, lanes // 2
    basis, occupied = masked.shape
    for b in range(mine_ref.shape[0]):
        for orbs_ref, core in ((mine_ref, core_ref[0]), (other_ref, 1 - core_ref[0])):
            rows = pl.ds(pl.multiple_of((2 * b + core) * BLK, BLK), BLK)
            keep = pattern_ref[2 * b + core].astype(F32)
            masked[rows, :] = (orbs_ref[b].astype(F32) * keep).astype(BF16)
    for s in range(0, height, step):
        halves = []
        for h in range(2):
            block = tensor_ref[:, h * height + s : h * height + s + step, :]
            value = jnp.dot(
                block.reshape(ri * step, basis), masked[...], preferred_element_type=F32
            )
            value = value.astype(BF16).reshape(ri, step, occupied)
            halves.append(pltpu.einshape("pmi->mpi", value))
        value = jnp.concatenate(halves, axis=1)
        turned = jnp.stack([value[m].T for m in range(step)])
        turned = pltpu.einshape("mjl->jml", turned)
        for i in range(2):
            first = i * height + s
            out_ref[:, first : first + step, :] = turned[i * owners : (i + 1) * owners]


def coeffs_of(core, pattern, mine, other, tensor3, owners, step=8):
    occupied = mine.shape[2]
    ri, mu, basis = tensor3.shape
    return pl.pallas_call(
        functools.partial(coeffs_kernel, step),
        out_shape=jax.ShapeDtypeStruct((owners, mu, 2 * ri), BF16),
        in_specs=[SMEM, SMEM, VMEM, VMEM, VMEM],
        out_specs=VMEM,
        scratch_shapes=[pltpu.VMEM((basis, occupied), BF16)],
        compiler_params=params(20),
        cost_estimate=pl.CostEstimate(
            flops=2 * tensor3.size * occupied, bytes_accessed=2 * tensor3.size, transcendentals=0
        ),
        name="coeffs",
    )(core, pattern, mine, other, tensor3)


def pack(coef_ref, out_ref):
    wide, blocks, orbitals, half, lanes = coef_ref.shape
    height, width = blocks * half, wide * lanes // 2
    low = lax.broadcasted_iota(jnp.int32, (height, lanes), 1) < lanes // 2
    for i in range(orbitals):
        for g in range(wide // 2):
            x = coef_ref[2 * g, :, i].reshape(height, lanes)
            y = coef_ref[2 * g + 1, :, i].reshape(height, lanes)
            one = jnp.where(low, x, pltpu.roll(y, lanes // 2, 1)).reshape(blocks, 1, half, lanes)
            two = jnp.where(low, pltpu.roll(x, lanes // 2, 1), y).reshape(blocks, 1, half, lanes)
            at = i * width + g * lanes
            both = jnp.concatenate([one, two], axis=1).reshape(2 * height, lanes)
            out_ref[:, at : at + lanes] = both


def coded(term, axis):
    largest = jnp.max(jnp.abs(term), axis=axis, keepdims=True)
    code = jnp.ceil(jnp.log2(jnp.maximum(largest, 1e-33)) * 256.0)
    return code, term * (jnp.exp2(code * (-1.0 / 256.0)) * TOP)


def term_of(core, first, count, packed_ref, metric_ref):
    width = metric_ref.shape[0]
    orbitals = packed_ref.shape[1] // width
    mine = packed_ref[first : first + count, :].astype(F32)
    mine = mine.reshape(count // 16, 2, 8, orbitals * width)
    mine = jnp.where(core == 0, mine[:, 0], mine[:, 1]).reshape(count // 2, orbitals * width)
    mine = mine.astype(BF16)
    fits = [
        lax.dot_general(
            mine[:, i * width : (i + 1) * width], metric_ref[...], NT, preferred_element_type=F32
        ).astype(BF16)
        for i in range(orbitals)
    ]
    fit = jnp.concatenate(fits, axis=1)
    return lax.dot_general(fit, packed_ref[...], NT, preferred_element_type=F32)


def partner_kernel(core_ref, coef_ref, metric_ref, packed_ref, out_ref):
    pack(coef_ref, packed_ref)
    term = term_of(1 - core_ref[0], 0, packed_ref.shape[0], packed_ref, metric_ref)
    columns = term.shape[1]
    code, scaled = coded(term, 1)
    out_ref[:, :columns] = jnp.round(scaled).astype(jnp.int32).astype(jnp.int16)
    tail = (term.shape[0], out_ref.shape[1] - columns)
    out_ref[:, columns:] = jnp.broadcast_to(code.astype(jnp.int32), tail).astype(jnp.int16)


def own_kernel(core_ref, packed_ref, metric_ref, out_ref):
    out_ref[...] = term_of(core_ref[0], 0, packed_ref.shape[0], packed_ref, metric_ref)


def term_call(kernel, name, out_shape, core, coef, metric):
    width = metric.shape[0]
    columns = coef.size // (2 * width)
    flops = 2 * columns * width * (width + columns)
    return pl.pallas_call(
        kernel,
        out_shape=out_shape,
        in_specs=[SMEM, VMEM, VMEM],
        out_specs=jax.tree.map(lambda _: VMEM, out_shape),
        compiler_params=params(20),
        cost_estimate=pl.CostEstimate(flops=flops, bytes_accessed=6 << 20, transcendentals=0),
        name=name,
    )(core, coef, metric)


def code_kernel(core_ref, sum_ref, held, out_ref):
    core = core_ref[0]
    blocks, rows, columns = out_ref.shape
    lanes = 128
    group = lanes // (2 * rows)
    shape = (group, rows, lanes)
    block = lax.broadcasted_iota(jnp.int32, shape, 0)
    row = lax.broadcasted_iota(jnp.int32, shape, 1)
    column = lax.broadcasted_iota(jnp.int32, shape, 2) - rows * (2 * block + core)
    first = (column == 0) & (row > 0)
    second = (column == 1) & (row == rows - 1)
    for g in range(blocks // group):
        some = slice(g * group * rows, (g + 1) * group * rows)
        other = held[some, :columns].astype(jnp.int32).astype(F32)
        power = held[some, columns : columns + 1].astype(jnp.int32).astype(F32)
        term = sum_ref[some, :] + other * (jnp.exp2(power * (1.0 / 256.0)) * (1.0 / TOP))
        term = term.reshape(group, rows, columns)
        code, scaled = coded(term, 2)
        part = scaled[:, :, g * lanes : (g + 1) * lanes]
        part = jnp.where(first, code, jnp.where(second, code[:, 0:1], part))
        scaled = [scaled[:, :, : g * lanes], part, scaled[:, :, (g + 1) * lanes :]]
        scaled = jnp.concatenate([piece for piece in scaled if piece.size], axis=2)
        out_ref[g * group : (g + 1) * group] = jnp.round(scaled).astype(jnp.int32).astype(jnp.int16)


def code_of(core, total, other, blocks):
    rows, columns = total.shape
    return pl.pallas_call(
        code_kernel,
        out_shape=jax.ShapeDtypeStruct((blocks, rows // blocks, columns), jnp.int16),
        in_specs=[SMEM, VMEM, VMEM],
        out_specs=VMEM,
        compiler_params=params(16),
        cost_estimate=pl.CostEstimate(flops=0, bytes_accessed=6 << 20, transcendentals=0),
        name="code",
    )(core, total, other)


def finish_kernel(me_ref, got_ref, out_ref):
    blocks, rows, columns = got_ref.shape
    lanes = 128
    start = rows * me_ref[0]
    base = pl.multiple_of(start // lanes * lanes, lanes)
    at = start - base
    window = got_ref[:, :, pl.ds(base, lanes)].astype(jnp.int32).astype(F32)
    lane = lax.broadcasted_iota(jnp.int32, window.shape, 2)
    row = lax.broadcasted_iota(jnp.int32, window.shape, 1)
    code = jnp.sum(jnp.where(lane == at, window, 0.0), axis=2, keepdims=True)
    other = jnp.sum(jnp.where(lane == at + 1, window, 0.0), axis=2, keepdims=True)
    code = jnp.where(row[:, :, :1] == 0, other[:, rows - 1 :], code)
    factor = jnp.exp2(code * (1.0 / 256.0)) * (-1.0 / TOP)
    total = jnp.zeros((rows, columns), F32)
    for s in range(blocks):
        total += got_ref[s].astype(jnp.int32).astype(F32) * factor[s]
    out_ref[...] = total
    part = out_ref[:, pl.ds(base, lanes)]
    lane = lax.broadcasted_iota(jnp.int32, part.shape, 1) - at
    row = lax.broadcasted_iota(jnp.int32, part.shape, 0)
    first = jnp.broadcast_to(part[0:1], part.shape)
    mirrored = jnp.sum(jnp.where(lane == row, first, 0.0), axis=1, keepdims=True)
    corner = jnp.sum(jnp.where((lane == rows - 1) & (row == 1), part, 0.0))
    part = jnp.where((lane == 0) & (row > 0), mirrored, part)
    out_ref[:, pl.ds(base, lanes)] = jnp.where((lane == 1) & (row == rows - 1), corner, part)


def finish(me, got):
    return pl.pallas_call(
        finish_kernel,
        out_shape=jax.ShapeDtypeStruct(got.shape[1:], F32),
        in_specs=[SMEM, VMEM],
        out_specs=VMEM,
        compiler_params=params(8),
        name="finish",
    )(me, got)


def body(tensor3, pattern, orbitals, metric):
    ri_local, mu_local, basis = tensor3.shape
    n_wide, n_narrow = lax.axis_size("wide"), lax.axis_size("narrow")
    devices = n_wide * n_narrow
    me = (lax.axis_index("wide") * n_narrow + lax.axis_index("narrow")).astype(jnp.int32)
    core = (lax.axis_index("narrow") & 1).astype(jnp.int32).reshape(1)
    me, core, orbitals = lax.optimization_barrier((me.reshape(1), core, orbitals))
    swap = [(i, i ^ 1) for i in range(n_narrow)]
    sides = [[i for i in range(n_narrow) if i % 2 == c] for c in (0, 1)]
    copies = copies_of(orbitals, n_narrow // 2)
    mine = lax.all_to_all(copies, "narrow", 0, 0, tiled=True, axis_index_groups=sides)
    other = lax.ppermute(mine, "narrow", swap)
    parts = coeffs_of(core, pattern.reshape(-1), mine, other, tensor3, devices)
    coef = lax.all_to_all(parts, BOTH, 0, 0, tiled=True)
    coef = coef.reshape(n_wide, n_narrow, 2, mu_local // 2, 2 * ri_local)
    mu = n_narrow * mu_local
    packed = jax.ShapeDtypeStruct((mu, 2 * metric.shape[0]), BF16)
    part = jax.ShapeDtypeStruct((mu // 2, mu + 128), jnp.int16)
    packed, other = term_call(partner_kernel, "partner", (packed, part), core, coef, metric)
    other = lax.ppermute(other, "narrow", swap)
    total = jax.ShapeDtypeStruct((mu // 2, mu), F32)
    total = term_call(own_kernel, "own", total, core, packed, metric)
    parts = code_of(core, total, other, devices // 2)
    sides = [[j for j in range(devices) if j % 2 == c] for c in (0, 1)]
    got = lax.all_to_all(parts, BOTH, 0, 0, tiled=True, axis_index_groups=sides)
    return finish(me, got)


def solution(mesh):
    in_specs = (P("wide", "narrow", None), P("wide", "narrow", None), P("narrow", None), P())
    out_specs = P(("wide", "narrow"), None)
    return jax.shard_map(body, mesh=mesh, in_specs=in_specs, out_specs=out_specs, check_vma=False)
```

```python
import functools

import jax
import jax.numpy as jnp
from jax import lax
from jax.experimental import pallas as pl
from jax.experimental.pallas import tpu as pltpu
from jax.sharding import PartitionSpec as P

BLK = 64
BOTH = ("wide", "narrow")
BF16, F32 = jnp.bfloat16, jnp.float32
TOP = 32766.0
VMEM = pl.BlockSpec(memory_space=pltpu.VMEM)
SMEM = pl.BlockSpec(memory_space=pltpu.SMEM)
NT = (((1,), (1,)), ((), ()))


def params(mib):
    return pltpu.CompilerParams(vmem_limit_bytes=mib << 20)


def copies_kernel(orbitals_ref, out_ref, sems):
    copies = [
        pltpu.make_async_copy(orbitals_ref, out_ref.at[i], sems.at[i])
        for i in range(out_ref.shape[0])
    ]
    for copy in copies:
        copy.start()
    for copy in copies:
        copy.wait()


def copies_of(orbitals, count):
    return pl.pallas_call(
        copies_kernel,
        out_shape=jax.ShapeDtypeStruct((count, *orbitals.shape), BF16),
        in_specs=[pl.BlockSpec(memory_space=pl.ANY)],
        out_specs=pl.BlockSpec(memory_space=pl.ANY),
        scratch_shapes=[pltpu.SemaphoreType.DMA((count,))],
        compiler_params=params(8),
        cost_estimate=pl.CostEstimate(flops=10**10, bytes_accessed=40 << 20, transcendentals=0),
        name="copies",
    )(pltpu.with_memory_space_constraint(orbitals, pltpu.HBM))


def coeffs_kernel(step, core_ref, pattern_ref, mine_ref, other_ref, tensor_ref, out_ref, masked):
    owners, height, lanes = out_ref.shape
    height, ri = height // 2, lanes // 2
    basis, occupied = masked.shape
    for b in range(mine_ref.shape[0]):
        for orbs_ref, core in ((mine_ref, core_ref[0]), (other_ref, 1 - core_ref[0])):
            rows = pl.ds(pl.multiple_of((2 * b + core) * BLK, BLK), BLK)
            keep = pattern_ref[2 * b + core].astype(F32)
            masked[rows, :] = (orbs_ref[b].astype(F32) * keep).astype(BF16)
    for s in range(0, height, step):
        halves = []
        for h in range(2):
            block = tensor_ref[:, h * height + s : h * height + s + step, :]
            value = jnp.dot(
                block.reshape(ri * step, basis), masked[...], preferred_element_type=F32
            )
            value = value.astype(BF16).reshape(ri, step, occupied)
            halves.append(pltpu.einshape("pmi->mpi", value))
        value = jnp.concatenate(halves, axis=1)
        turned = jnp.stack([value[m].T for m in range(step)])
        turned = pltpu.einshape("mjl->jml", turned)
        for i in range(2):
            first = i * height + s
            out_ref[:, first : first + step, :] = turned[i * owners : (i + 1) * owners]


def coeffs_of(core, pattern, mine, other, tensor3, owners, step=8):
    occupied = mine.shape[2]
    ri, mu, basis = tensor3.shape
    return pl.pallas_call(
        functools.partial(coeffs_kernel, step),
        out_shape=jax.ShapeDtypeStruct((owners, mu, 2 * ri), BF16),
        in_specs=[SMEM, SMEM, VMEM, VMEM, VMEM],
        out_specs=VMEM,
        scratch_shapes=[pltpu.VMEM((basis, occupied), BF16)],
        compiler_params=params(20),
        cost_estimate=pl.CostEstimate(
            flops=2 * tensor3.size * occupied, bytes_accessed=2 * tensor3.size, transcendentals=0
        ),
        name="coeffs",
    )(core, pattern, mine, other, tensor3)


def pack(coef_ref, out_ref):
    wide, blocks, orbitals, half, lanes = coef_ref.shape
    height, width = blocks * half, wide * lanes // 2
    low = lax.broadcasted_iota(jnp.int32, (height, lanes), 1) < lanes // 2
    for i in range(orbitals):
        for g in range(wide // 2):
            x = coef_ref[2 * g, :, i].reshape(height, lanes)
            y = coef_ref[2 * g + 1, :, i].reshape(height, lanes)
            one = jnp.where(low, x, pltpu.roll(y, lanes // 2, 1)).reshape(blocks, 1, half, lanes)
            two = jnp.where(low, pltpu.roll(x, lanes // 2, 1), y).reshape(blocks, 1, half, lanes)
            at = i * width + g * lanes
            both = jnp.concatenate([one, two], axis=1).reshape(2 * height, lanes)
            out_ref[:, at : at + lanes] = both


def coded(term, axis):
    largest = jnp.max(jnp.abs(term), axis=axis, keepdims=True)
    code = jnp.ceil(jnp.log2(jnp.maximum(largest, 1e-33)) * 256.0)
    return code, term * (jnp.exp2(code * (-1.0 / 256.0)) * TOP)


def term_of(core, first, count, packed_ref, metric_ref):
    width = metric_ref.shape[0]
    orbitals = packed_ref.shape[1] // width
    mine = packed_ref[first : first + count, :].astype(F32)
    mine = mine.reshape(count // 16, 2, 8, orbitals * width)
    mine = jnp.where(core == 0, mine[:, 0], mine[:, 1]).reshape(count // 2, orbitals * width)
    mine = mine.astype(BF16)
    fits = [
        lax.dot_general(
            mine[:, i * width : (i + 1) * width], metric_ref[...], NT, preferred_element_type=F32
        ).astype(BF16)
        for i in range(orbitals)
    ]
    fit = jnp.concatenate(fits, axis=1)
    return lax.dot_general(fit, packed_ref[...], NT, preferred_element_type=F32)


def partner_kernel(core_ref, coef_ref, metric_ref, packed_ref, *out_refs):
    pack(coef_ref, packed_ref)
    term = term_of(1 - core_ref[0], 0, packed_ref.shape[0], packed_ref, metric_ref)
    columns = term.shape[1]
    code, scaled = coded(term, 1)
    tail = (term.shape[0], out_refs[0].shape[1] - columns)
    scaled = jnp.concatenate([jnp.round(scaled), jnp.broadcast_to(code, tail)], axis=1)
    scaled = scaled.astype(jnp.int32).astype(jnp.int16)
    rows = out_refs[0].shape[0]
    for k, out_ref in enumerate(out_refs):
        out_ref[...] = scaled[k * rows : (k + 1) * rows]


def own_kernel(core_ref, packed_ref, metric_ref, out_ref):
    out_ref[...] = term_of(core_ref[0], 0, packed_ref.shape[0], packed_ref, metric_ref)


def term_call(kernel, name, out_shape, core, coef, metric):
    width = metric.shape[0]
    columns = coef.size // (2 * width)
    flops = 2 * columns * width * (width + columns)
    return pl.pallas_call(
        kernel,
        out_shape=out_shape,
        in_specs=[SMEM, VMEM, VMEM],
        out_specs=jax.tree.map(lambda _: VMEM, out_shape),
        compiler_params=params(20),
        cost_estimate=pl.CostEstimate(flops=flops, bytes_accessed=6 << 20, transcendentals=0),
        name=name,
    )(core, coef, metric)


def code_kernel(core_ref, sum_ref, one_ref, two_ref, out_ref):
    core = core_ref[0]
    blocks, rows, columns = out_ref.shape
    lanes = 128
    group = lanes // (2 * rows)
    shape = (group, rows, lanes)
    block = lax.broadcasted_iota(jnp.int32, shape, 0)
    row = lax.broadcasted_iota(jnp.int32, shape, 1)
    column = lax.broadcasted_iota(jnp.int32, shape, 2) - rows * (2 * block + core)
    first = (column == 0) & (row > 0)
    second = (column == 1) & (row == rows - 1)
    for g in range(blocks // group):
        some = slice(g * group * rows, (g + 1) * group * rows)
        held = (one_ref, two_ref)[some.start // one_ref.shape[0]]
        first_row = some.start % one_ref.shape[0]
        there = slice(first_row, first_row + group * rows)
        other = held[there, :columns].astype(jnp.int32).astype(F32)
        power = held[there, columns : columns + 1].astype(jnp.int32).astype(F32)
        term = sum_ref[some, :] + other * (jnp.exp2(power * (1.0 / 256.0)) * (1.0 / TOP))
        term = term.reshape(group, rows, columns)
        code, scaled = coded(term, 2)
        part = scaled[:, :, g * lanes : (g + 1) * lanes]
        part = jnp.where(first, code, jnp.where(second, code[:, 0:1], part))
        scaled = [scaled[:, :, : g * lanes], part, scaled[:, :, (g + 1) * lanes :]]
        scaled = jnp.concatenate([piece for piece in scaled if piece.size], axis=2)
        out_ref[g * group : (g + 1) * group] = jnp.round(scaled).astype(jnp.int32).astype(jnp.int16)


def code_of(core, total, others, blocks):
    rows, columns = total.shape
    return pl.pallas_call(
        code_kernel,
        out_shape=jax.ShapeDtypeStruct((blocks, rows // blocks, columns), jnp.int16),
        in_specs=[SMEM, VMEM, VMEM, VMEM],
        out_specs=VMEM,
        compiler_params=params(16),
        cost_estimate=pl.CostEstimate(flops=0, bytes_accessed=6 << 20, transcendentals=0),
        name="code",
    )(core, total, *others)


def finish_kernel(me_ref, got_ref, out_ref):
    blocks, rows, columns = got_ref.shape
    lanes = 128
    start = rows * me_ref[0]
    base = pl.multiple_of(start // lanes * lanes, lanes)
    at = start - base
    window = got_ref[:, :, pl.ds(base, lanes)].astype(jnp.int32).astype(F32)
    lane = lax.broadcasted_iota(jnp.int32, window.shape, 2)
    row = lax.broadcasted_iota(jnp.int32, window.shape, 1)
    code = jnp.sum(jnp.where(lane == at, window, 0.0), axis=2, keepdims=True)
    other = jnp.sum(jnp.where(lane == at + 1, window, 0.0), axis=2, keepdims=True)
    code = jnp.where(row[:, :, :1] == 0, other[:, rows - 1 :], code)
    factor = jnp.exp2(code * (1.0 / 256.0)) * (-1.0 / TOP)
    total = jnp.zeros((rows, columns), F32)
    for s in range(blocks):
        total += got_ref[s].astype(jnp.int32).astype(F32) * factor[s]
    out_ref[...] = total
    part = out_ref[:, pl.ds(base, lanes)]
    lane = lax.broadcasted_iota(jnp.int32, part.shape, 1) - at
    row = lax.broadcasted_iota(jnp.int32, part.shape, 0)
    first = jnp.broadcast_to(part[0:1], part.shape)
    mirrored = jnp.sum(jnp.where(lane == row, first, 0.0), axis=1, keepdims=True)
    corner = jnp.sum(jnp.where((lane == rows - 1) & (row == 1), part, 0.0))
    part = jnp.where((lane == 0) & (row > 0), mirrored, part)
    out_ref[:, pl.ds(base, lanes)] = jnp.where((lane == 1) & (row == rows - 1), corner, part)


def finish(me, got):
    return pl.pallas_call(
        finish_kernel,
        out_shape=jax.ShapeDtypeStruct(got.shape[1:], F32),
        in_specs=[SMEM, VMEM],
        out_specs=VMEM,
        compiler_params=params(8),
        name="finish",
    )(me, got)


def body(tensor3, pattern, orbitals, metric):
    ri_local, mu_local, basis = tensor3.shape
    n_wide, n_narrow = lax.axis_size("wide"), lax.axis_size("narrow")
    devices = n_wide * n_narrow
    me = (lax.axis_index("wide") * n_narrow + lax.axis_index("narrow")).astype(jnp.int32)
    core = (lax.axis_index("narrow") & 1).astype(jnp.int32).reshape(1)
    me, core, orbitals = lax.optimization_barrier((me.reshape(1), core, orbitals))
    swap = [(i, i ^ 1) for i in range(n_narrow)]
    sides = [[i for i in range(n_narrow) if i % 2 == c] for c in (0, 1)]
    copies = copies_of(orbitals, n_narrow // 2)
    mine = lax.all_to_all(copies, "narrow", 0, 0, tiled=True, axis_index_groups=sides)
    other = lax.ppermute(mine, "narrow", swap)
    parts = coeffs_of(core, pattern.reshape(-1), mine, other, tensor3, devices)
    coef = lax.all_to_all(parts, BOTH, 0, 0, tiled=True)
    coef = coef.reshape(n_wide, n_narrow, 2, mu_local // 2, 2 * ri_local)
    mu = n_narrow * mu_local
    packed = jax.ShapeDtypeStruct((mu, 2 * metric.shape[0]), BF16)
    part = jax.ShapeDtypeStruct((mu // 4, mu + 128), jnp.int16)
    packed, *others = term_call(partner_kernel, "partner", (packed, part, part), core, coef, metric)
    others = [lax.ppermute(part, "narrow", swap) for part in others]
    total = jax.ShapeDtypeStruct((mu // 2, mu), F32)
    total = term_call(own_kernel, "own", total, core, packed, metric)
    parts = code_of(core, total, others, devices // 2)
    sides = [[j for j in range(devices) if j % 2 == c] for c in (0, 1)]
    got = lax.all_to_all(parts, BOTH, 0, 0, tiled=True, axis_index_groups=sides)
    return finish(me, got)


def solution(mesh):
    in_specs = (P("wide", "narrow", None), P("wide", "narrow", None), P("narrow", None), P())
    out_specs = P(("wide", "narrow"), None)
    return jax.shard_map(body, mesh=mesh, in_specs=in_specs, out_specs=out_specs, check_vma=False)
```

```python
import functools

import jax
import jax.numpy as jnp
from jax import lax
from jax.experimental import pallas as pl
from jax.experimental.pallas import tpu as pltpu
from jax.sharding import PartitionSpec as P

BLK = 64
BOTH = ("wide", "narrow")
BF16, F32 = jnp.bfloat16, jnp.float32
TOP = 32766.0
VMEM = pl.BlockSpec(memory_space=pltpu.VMEM)
SMEM = pl.BlockSpec(memory_space=pltpu.SMEM)
NT = (((1,), (1,)), ((), ()))


def params(mib):
    return pltpu.CompilerParams(vmem_limit_bytes=mib << 20)


def copies_kernel(orbitals_ref, out_ref, held, sem):
    copy = pltpu.make_async_copy(orbitals_ref, held, sem)
    copy.start()
    copy.wait()
    value = held[...]
    for i in range(out_ref.shape[0]):
        out_ref[i] = value


def copies_of(orbitals, count):
    return pl.pallas_call(
        copies_kernel,
        out_shape=jax.ShapeDtypeStruct((count, *orbitals.shape), BF16),
        in_specs=[pl.BlockSpec(memory_space=pl.ANY)],
        out_specs=VMEM,
        scratch_shapes=[pltpu.VMEM(orbitals.shape, BF16), pltpu.SemaphoreType.DMA],
        compiler_params=params(8),
        cost_estimate=pl.CostEstimate(flops=10**10, bytes_accessed=40 << 20, transcendentals=0),
        name="copies",
    )(pltpu.with_memory_space_constraint(orbitals, pltpu.HBM))


def coeffs_kernel(step, core_ref, pattern_ref, mine_ref, other_ref, tensor_ref, out_ref, masked):
    owners, height, lanes = out_ref.shape
    height, ri = height // 2, lanes // 2
    basis, occupied = masked.shape
    for b in range(mine_ref.shape[0]):
        for orbs_ref, core in ((mine_ref, core_ref[0]), (other_ref, 1 - core_ref[0])):
            rows = pl.ds(pl.multiple_of((2 * b + core) * BLK, BLK), BLK)
            keep = pattern_ref[2 * b + core].astype(F32)
            masked[rows, :] = (orbs_ref[b].astype(F32) * keep).astype(BF16)
    for s in range(0, height, step):
        halves = []
        for h in range(2):
            block = tensor_ref[:, h * height + s : h * height + s + step, :]
            value = jnp.dot(
                block.reshape(ri * step, basis), masked[...], preferred_element_type=F32
            )
            value = value.astype(BF16).reshape(ri, step, occupied)
            halves.append(pltpu.einshape("pmi->mpi", value))
        value = jnp.concatenate(halves, axis=1)
        turned = jnp.stack([value[m].T for m in range(step)])
        turned = pltpu.einshape("mjl->jml", turned)
        for i in range(2):
            first = i * height + s
            out_ref[:, first : first + step, :] = turned[i * owners : (i + 1) * owners]


def coeffs_of(core, pattern, mine, other, tensor3, owners, step=8):
    occupied = mine.shape[2]
    ri, mu, basis = tensor3.shape
    return pl.pallas_call(
        functools.partial(coeffs_kernel, step),
        out_shape=jax.ShapeDtypeStruct((owners, mu, 2 * ri), BF16),
        in_specs=[SMEM, SMEM, VMEM, VMEM, VMEM],
        out_specs=VMEM,
        scratch_shapes=[pltpu.VMEM((basis, occupied), BF16)],
        compiler_params=params(20),
        cost_estimate=pl.CostEstimate(
            flops=2 * tensor3.size * occupied, bytes_accessed=2 * tensor3.size, transcendentals=0
        ),
        name="coeffs",
    )(core, pattern, mine, other, tensor3)


def pack(coef_ref, out_ref):
    wide, blocks, orbitals, half, lanes = coef_ref.shape
    height, width = blocks * half, wide * lanes // 2
    low = lax.broadcasted_iota(jnp.int32, (height, lanes), 1) < lanes // 2
    for i in range(orbitals):
        for g in range(wide // 2):
            x = coef_ref[2 * g, :, i].reshape(height, lanes)
            y = coef_ref[2 * g + 1, :, i].reshape(height, lanes)
            one = jnp.where(low, x, pltpu.roll(y, lanes // 2, 1)).reshape(blocks, 1, half, lanes)
            two = jnp.where(low, pltpu.roll(x, lanes // 2, 1), y).reshape(blocks, 1, half, lanes)
            at = i * width + g * lanes
            both = jnp.concatenate([one, two], axis=1).reshape(2 * height, lanes)
            out_ref[:, at : at + lanes] = both


def coded(term, axis):
    largest = jnp.max(jnp.abs(term), axis=axis, keepdims=True)
    code = jnp.ceil(jnp.log2(jnp.maximum(largest, 1e-33)) * 256.0)
    return code, term * (jnp.exp2(code * (-1.0 / 256.0)) * TOP)


def term_of(core, first, count, packed_ref, metric_ref):
    width = metric_ref.shape[0]
    orbitals = packed_ref.shape[1] // width
    mine = packed_ref[first : first + count, :].astype(F32)
    mine = mine.reshape(count // 16, 2, 8, orbitals * width)
    mine = jnp.where(core == 0, mine[:, 0], mine[:, 1]).reshape(count // 2, orbitals * width)
    mine = mine.astype(BF16)
    fits = [
        lax.dot_general(
            mine[:, i * width : (i + 1) * width], metric_ref[...], NT, preferred_element_type=F32
        ).astype(BF16)
        for i in range(orbitals)
    ]
    fit = jnp.concatenate(fits, axis=1)
    return lax.dot_general(fit, packed_ref[...], NT, preferred_element_type=F32)


def partner_kernel(core_ref, coef_ref, metric_ref, packed_ref, out_ref):
    pack(coef_ref, packed_ref)
    term = term_of(1 - core_ref[0], 0, packed_ref.shape[0], packed_ref, metric_ref)
    columns = term.shape[1]
    code, scaled = coded(term, 1)
    out_ref[:, :columns] = jnp.round(scaled).astype(jnp.int32).astype(jnp.int16)
    tail = (term.shape[0], out_ref.shape[1] - columns)
    out_ref[:, columns:] = jnp.broadcast_to(code.astype(jnp.int32), tail).astype(jnp.int16)


def own_kernel(core_ref, packed_ref, metric_ref, out_ref):
    out_ref[...] = term_of(core_ref[0], 0, packed_ref.shape[0], packed_ref, metric_ref)


def term_call(kernel, name, out_shape, core, coef, metric):
    width = metric.shape[0]
    columns = coef.size // (2 * width)
    flops = 2 * columns * width * (width + columns)
    return pl.pallas_call(
        kernel,
        out_shape=out_shape,
        in_specs=[SMEM, VMEM, VMEM],
        out_specs=jax.tree.map(lambda _: VMEM, out_shape),
        compiler_params=params(20),
        cost_estimate=pl.CostEstimate(flops=flops, bytes_accessed=6 << 20, transcendentals=0),
        name=name,
    )(core, coef, metric)


def code_kernel(core_ref, sum_ref, held, out_ref):
    core = core_ref[0]
    blocks, rows, columns = out_ref.shape
    lanes = 128
    group = lanes // (2 * rows)
    shape = (group, rows, lanes)
    block = lax.broadcasted_iota(jnp.int32, shape, 0)
    row = lax.broadcasted_iota(jnp.int32, shape, 1)
    column = lax.broadcasted_iota(jnp.int32, shape, 2) - rows * (2 * block + core)
    first = (column == 0) & (row > 0)
    second = (column == 1) & (row == rows - 1)
    for g in range(blocks // group):
        some = slice(g * group * rows, (g + 1) * group * rows)
        other = held[some, :columns].astype(jnp.int32).astype(F32)
        power = held[some, columns : columns + 1].astype(jnp.int32).astype(F32)
        term = sum_ref[some, :] + other * (jnp.exp2(power * (1.0 / 256.0)) * (1.0 / TOP))
        term = term.reshape(group, rows, columns)
        code, scaled = coded(term, 2)
        part = scaled[:, :, g * lanes : (g + 1) * lanes]
        part = jnp.where(first, code, jnp.where(second, code[:, 0:1], part))
        scaled = [scaled[:, :, : g * lanes], part, scaled[:, :, (g + 1) * lanes :]]
        scaled = jnp.concatenate([piece for piece in scaled if piece.size], axis=2)
        out_ref[g * group : (g + 1) * group] = jnp.round(scaled).astype(jnp.int32).astype(jnp.int16)


def code_of(core, total, other, blocks):
    rows, columns = total.shape
    return pl.pallas_call(
        code_kernel,
        out_shape=jax.ShapeDtypeStruct((blocks, rows // blocks, columns), jnp.int16),
        in_specs=[SMEM, VMEM, VMEM],
        out_specs=VMEM,
        compiler_params=params(16),
        cost_estimate=pl.CostEstimate(flops=0, bytes_accessed=6 << 20, transcendentals=0),
        name="code",
    )(core, total, other)


def finish_kernel(me_ref, got_ref, out_ref):
    blocks, rows, columns = got_ref.shape
    lanes = 128
    start = rows * me_ref[0]
    base = pl.multiple_of(start // lanes * lanes, lanes)
    at = start - base
    window = got_ref[:, :, pl.ds(base, lanes)].astype(jnp.int32).astype(F32)
    lane = lax.broadcasted_iota(jnp.int32, window.shape, 2)
    row = lax.broadcasted_iota(jnp.int32, window.shape, 1)
    code = jnp.sum(jnp.where(lane == at, window, 0.0), axis=2, keepdims=True)
    other = jnp.sum(jnp.where(lane == at + 1, window, 0.0), axis=2, keepdims=True)
    code = jnp.where(row[:, :, :1] == 0, other[:, rows - 1 :], code)
    factor = jnp.exp2(code * (1.0 / 256.0)) * (-1.0 / TOP)
    total = jnp.zeros((rows, columns), F32)
    for s in range(blocks):
        total += got_ref[s].astype(jnp.int32).astype(F32) * factor[s]
    out_ref[...] = total
    part = out_ref[:, pl.ds(base, lanes)]
    lane = lax.broadcasted_iota(jnp.int32, part.shape, 1) - at
    row = lax.broadcasted_iota(jnp.int32, part.shape, 0)
    first = jnp.broadcast_to(part[0:1], part.shape)
    mirrored = jnp.sum(jnp.where(lane == row, first, 0.0), axis=1, keepdims=True)
    corner = jnp.sum(jnp.where((lane == rows - 1) & (row == 1), part, 0.0))
    part = jnp.where((lane == 0) & (row > 0), mirrored, part)
    out_ref[:, pl.ds(base, lanes)] = jnp.where((lane == 1) & (row == rows - 1), corner, part)


def finish(me, got):
    return pl.pallas_call(
        finish_kernel,
        out_shape=jax.ShapeDtypeStruct(got.shape[1:], F32),
        in_specs=[SMEM, VMEM],
        out_specs=VMEM,
        compiler_params=params(8),
        name="finish",
    )(me, got)


def body(tensor3, pattern, orbitals, metric):
    ri_local, mu_local, basis = tensor3.shape
    n_wide, n_narrow = lax.axis_size("wide"), lax.axis_size("narrow")
    devices = n_wide * n_narrow
    me = (lax.axis_index("wide") * n_narrow + lax.axis_index("narrow")).astype(jnp.int32)
    core = (lax.axis_index("narrow") & 1).astype(jnp.int32).reshape(1)
    me, core, orbitals = lax.optimization_barrier((me.reshape(1), core, orbitals))
    swap = [(i, i ^ 1) for i in range(n_narrow)]
    sides = [[i for i in range(n_narrow) if i % 2 == c] for c in (0, 1)]
    copies = copies_of(orbitals, n_narrow // 2)
    mine = lax.all_to_all(copies, "narrow", 0, 0, tiled=True, axis_index_groups=sides)
    other = lax.ppermute(mine, "narrow", swap)
    parts = coeffs_of(core, pattern.reshape(-1), mine, other, tensor3, devices)
    coef = lax.all_to_all(parts, BOTH, 0, 0, tiled=True)
    coef = coef.reshape(n_wide, n_narrow, 2, mu_local // 2, 2 * ri_local)
    mu = n_narrow * mu_local
    packed = jax.ShapeDtypeStruct((mu, 2 * metric.shape[0]), BF16)
    part = jax.ShapeDtypeStruct((mu // 2, mu + 128), jnp.int16)
    packed, other = term_call(partner_kernel, "partner", (packed, part), core, coef, metric)
    other = lax.ppermute(other, "narrow", swap)
    total = jax.ShapeDtypeStruct((mu // 2, mu), F32)
    total = term_call(own_kernel, "own", total, core, packed, metric)
    parts = code_of(core, total, other, devices // 2)
    sides = [[j for j in range(devices) if j % 2 == c] for c in (0, 1)]
    got = lax.all_to_all(parts, BOTH, 0, 0, tiled=True, axis_index_groups=sides)
    return finish(me, got)


def solution(mesh):
    in_specs = (P("wide", "narrow", None), P("wide", "narrow", None), P("narrow", None), P())
    out_specs = P(("wide", "narrow"), None)
    return jax.shard_map(body, mesh=mesh, in_specs=in_specs, out_specs=out_specs, check_vma=False)
```

```python
import functools

import jax
import jax.numpy as jnp
from jax import lax
from jax.experimental import pallas as pl
from jax.experimental.pallas import tpu as pltpu
from jax.sharding import PartitionSpec as P

BLK = 64
BOTH = ("wide", "narrow")
BF16, F32 = jnp.bfloat16, jnp.float32
TOP = 32766.0
VMEM = pl.BlockSpec(memory_space=pltpu.VMEM)
SMEM = pl.BlockSpec(memory_space=pltpu.SMEM)
NT = (((1,), (1,)), ((), ()))


def params(mib):
    return pltpu.CompilerParams(vmem_limit_bytes=mib << 20)


def copies_kernel(orbitals_ref, out_ref, held, sem):
    copy = pltpu.make_async_copy(orbitals_ref, held, sem)
    copy.start()
    copy.wait()
    value = held[...]
    for i in range(out_ref.shape[0]):
        out_ref[i] = value


def copies_of(orbitals, count):
    return pl.pallas_call(
        copies_kernel,
        out_shape=jax.ShapeDtypeStruct((count, *orbitals.shape), BF16),
        in_specs=[pl.BlockSpec(memory_space=pl.ANY)],
        out_specs=VMEM,
        scratch_shapes=[pltpu.VMEM(orbitals.shape, BF16), pltpu.SemaphoreType.DMA],
        compiler_params=params(8),
        cost_estimate=pl.CostEstimate(flops=10**10, bytes_accessed=40 << 20, transcendentals=0),
        name="copies",
    )(pltpu.with_memory_space_constraint(orbitals, pltpu.HBM))


def coeffs_kernel(step, core_ref, pattern_ref, mine_ref, other_ref, tensor_ref, out_ref, masked):
    owners, height, lanes = out_ref.shape
    height, ri = height // 2, lanes // 2
    basis, occupied = masked.shape
    for b in range(mine_ref.shape[0]):
        for orbs_ref, core in ((mine_ref, core_ref[0]), (other_ref, 1 - core_ref[0])):
            rows = pl.ds(pl.multiple_of((2 * b + core) * BLK, BLK), BLK)
            keep = pattern_ref[2 * b + core].astype(F32)
            masked[rows, :] = (orbs_ref[b].astype(F32) * keep).astype(BF16)
    for s in range(0, height, step):
        halves = []
        for h in range(2):
            block = tensor_ref[:, h * height + s : h * height + s + step, :]
            value = jnp.dot(
                block.reshape(ri * step, basis), masked[...], preferred_element_type=F32
            )
            value = value.astype(BF16).reshape(ri, step, occupied)
            halves.append(pltpu.einshape("pmi->mpi", value))
        value = jnp.concatenate(halves, axis=1)
        turned = jnp.stack([value[m].T for m in range(step)])
        turned = pltpu.einshape("mjl->jml", turned)
        for i in range(2):
            first = i * height + s
            out_ref[:, first : first + step, :] = turned[i * owners : (i + 1) * owners]


def coeffs_of(core, pattern, mine, other, tensor3, owners, step=8):
    occupied = mine.shape[2]
    ri, mu, basis = tensor3.shape
    return pl.pallas_call(
        functools.partial(coeffs_kernel, step),
        out_shape=jax.ShapeDtypeStruct((owners, mu, 2 * ri), BF16),
        in_specs=[SMEM, SMEM, VMEM, VMEM, VMEM],
        out_specs=VMEM,
        scratch_shapes=[pltpu.VMEM((basis, occupied), BF16)],
        compiler_params=params(20),
        cost_estimate=pl.CostEstimate(
            flops=2 * tensor3.size * occupied, bytes_accessed=2 * tensor3.size, transcendentals=0
        ),
        name="coeffs",
    )(core, pattern, mine, other, tensor3)


def pack(coef_ref, out_ref):
    wide, blocks, orbitals, half, lanes = coef_ref.shape
    height, width = blocks * half, wide * lanes // 2
    low = lax.broadcasted_iota(jnp.int32, (height, lanes), 1) < lanes // 2
    for i in range(orbitals):
        for g in range(wide // 2):
            x = coef_ref[2 * g, :, i].reshape(height, lanes)
            y = coef_ref[2 * g + 1, :, i].reshape(height, lanes)
            one = jnp.where(low, x, pltpu.roll(y, lanes // 2, 1)).reshape(blocks, 1, half, lanes)
            two = jnp.where(low, pltpu.roll(x, lanes // 2, 1), y).reshape(blocks, 1, half, lanes)
            at = i * width + g * lanes
            both = jnp.concatenate([one, two], axis=1).reshape(2 * height, lanes)
            out_ref[:, at : at + lanes] = both


def coded(term, axis):
    largest = jnp.max(jnp.abs(term), axis=axis, keepdims=True)
    code = jnp.ceil(jnp.log2(jnp.maximum(largest, 1e-33)) * 256.0)
    return code, term * (jnp.exp2(code * (-1.0 / 256.0)) * TOP)


def term_of(core, first, count, packed_ref, metric_ref):
    width = metric_ref.shape[0]
    orbitals = packed_ref.shape[1] // width
    mine = packed_ref[first : first + count, :].astype(F32)
    mine = mine.reshape(count // 16, 2, 8, orbitals * width)
    mine = jnp.where(core == 0, mine[:, 0], mine[:, 1]).reshape(count // 2, orbitals * width)
    mine = mine.astype(BF16)
    fits = [
        lax.dot_general(
            mine[:, i * width : (i + 1) * width], metric_ref[...], NT, preferred_element_type=F32
        ).astype(BF16)
        for i in range(orbitals)
    ]
    fit = jnp.concatenate(fits, axis=1)
    return lax.dot_general(fit, packed_ref[...], NT, preferred_element_type=F32)


def partner_kernel(core_ref, coef_ref, metric_ref, packed_ref, out_ref):
    pack(coef_ref, packed_ref)
    term = term_of(1 - core_ref[0], 0, packed_ref.shape[0], packed_ref, metric_ref)
    columns = term.shape[1]
    code, scaled = coded(term, 1)
    out_ref[:, :columns] = jnp.round(scaled).astype(jnp.int32).astype(jnp.int16)
    tail = (term.shape[0], out_ref.shape[1] - columns)
    out_ref[:, columns:] = jnp.broadcast_to(code.astype(jnp.int32), tail).astype(jnp.int16)


def own_kernel(core_ref, packed_ref, metric_ref, out_ref):
    out_ref[...] = term_of(core_ref[0], 0, packed_ref.shape[0], packed_ref, metric_ref)


def term_call(kernel, name, out_shape, core, coef, metric):
    width = metric.shape[0]
    columns = coef.size // (2 * width)
    flops = 2 * columns * width * (width + columns)
    return pl.pallas_call(
        kernel,
        out_shape=out_shape,
        in_specs=[SMEM, VMEM, VMEM],
        out_specs=jax.tree.map(lambda _: VMEM, out_shape),
        compiler_params=params(20),
        cost_estimate=pl.CostEstimate(flops=flops, bytes_accessed=6 << 20, transcendentals=0),
        name=name,
    )(core, coef, metric)


def code_kernel(core_ref, sum_ref, held, out_ref):
    core = core_ref[0]
    blocks, rows, columns = out_ref.shape
    lanes = 128
    group = lanes // (2 * rows)
    shape = (group, rows, lanes)
    block = lax.broadcasted_iota(jnp.int32, shape, 0)
    row = lax.broadcasted_iota(jnp.int32, shape, 1)
    column = lax.broadcasted_iota(jnp.int32, shape, 2) - rows * (2 * block + core)
    first = (column == 0) & (row > 0)
    second = (column == 1) & (row == rows - 1)
    for g in range(blocks // group):
        some = slice(g * group * rows, (g + 1) * group * rows)
        other = held[some, :columns].astype(jnp.int32).astype(F32)
        power = held[some, columns : columns + 1].astype(jnp.int32).astype(F32)
        term = sum_ref[some, :] + other * (jnp.exp2(power * (1.0 / 256.0)) * (1.0 / TOP))
        term = term.reshape(group, rows, columns)
        code, scaled = coded(term, 2)
        part = scaled[:, :, g * lanes : (g + 1) * lanes]
        part = jnp.where(first, code, jnp.where(second, code[:, 0:1], part))
        scaled = [scaled[:, :, : g * lanes], part, scaled[:, :, (g + 1) * lanes :]]
        scaled = jnp.concatenate([piece for piece in scaled if piece.size], axis=2)
        out_ref[g * group : (g + 1) * group] = jnp.round(scaled).astype(jnp.int32).astype(jnp.int16)


def code_of(core, total, other, blocks):
    rows, columns = total.shape
    return pl.pallas_call(
        code_kernel,
        out_shape=jax.ShapeDtypeStruct((blocks, rows // blocks, columns), jnp.int16),
        in_specs=[SMEM, VMEM, VMEM],
        out_specs=VMEM,
        compiler_params=params(16),
        cost_estimate=pl.CostEstimate(flops=0, bytes_accessed=6 << 20, transcendentals=0),
        name="code",
    )(core, total, other)


def finish_kernel(me_ref, got_ref, out_ref):
    blocks, rows, columns = got_ref.shape
    lanes = 128
    start = rows * me_ref[0]
    base = pl.multiple_of(start // lanes * lanes, lanes)
    at = start - base
    window = got_ref[:, :, pl.ds(base, lanes)].astype(jnp.int32).astype(F32)
    lane = lax.broadcasted_iota(jnp.int32, window.shape, 2)
    row = lax.broadcasted_iota(jnp.int32, window.shape, 1)
    code = jnp.sum(jnp.where(lane == at, window, 0.0), axis=2, keepdims=True)
    other = jnp.sum(jnp.where(lane == at + 1, window, 0.0), axis=2, keepdims=True)
    code = jnp.where(row[:, :, :1] == 0, other[:, rows - 1 :], code)
    factor = jnp.exp2(code * (1.0 / 256.0)) * (-1.0 / TOP)
    sums = [jnp.zeros((rows, columns), F32) for _ in range(4)]
    for s in range(blocks):
        sums[s % 4] += got_ref[s].astype(jnp.int32).astype(F32) * factor[s]
    out_ref[...] = (sums[0] + sums[1]) + (sums[2] + sums[3])
    part = out_ref[:, pl.ds(base, lanes)]
    lane = lax.broadcasted_iota(jnp.int32, part.shape, 1) - at
    row = lax.broadcasted_iota(jnp.int32, part.shape, 0)
    first = jnp.broadcast_to(part[0:1], part.shape)
    mirrored = jnp.sum(jnp.where(lane == row, first, 0.0), axis=1, keepdims=True)
    corner = jnp.sum(jnp.where((lane == rows - 1) & (row == 1), part, 0.0))
    part = jnp.where((lane == 0) & (row > 0), mirrored, part)
    out_ref[:, pl.ds(base, lanes)] = jnp.where((lane == 1) & (row == rows - 1), corner, part)


def finish(me, got):
    return pl.pallas_call(
        finish_kernel,
        out_shape=jax.ShapeDtypeStruct(got.shape[1:], F32),
        in_specs=[SMEM, VMEM],
        out_specs=VMEM,
        compiler_params=params(8),
        name="finish",
    )(me, got)


def body(tensor3, pattern, orbitals, metric):
    ri_local, mu_local, basis = tensor3.shape
    n_wide, n_narrow = lax.axis_size("wide"), lax.axis_size("narrow")
    devices = n_wide * n_narrow
    me = (lax.axis_index("wide") * n_narrow + lax.axis_index("narrow")).astype(jnp.int32)
    core = (lax.axis_index("narrow") & 1).astype(jnp.int32).reshape(1)
    me, core, orbitals = lax.optimization_barrier((me.reshape(1), core, orbitals))
    swap = [(i, i ^ 1) for i in range(n_narrow)]
    sides = [[i for i in range(n_narrow) if i % 2 == c] for c in (0, 1)]
    copies = copies_of(orbitals, n_narrow // 2)
    mine = lax.all_to_all(copies, "narrow", 0, 0, tiled=True, axis_index_groups=sides)
    other = lax.ppermute(mine, "narrow", swap)
    parts = coeffs_of(core, pattern.reshape(-1), mine, other, tensor3, devices)
    coef = lax.all_to_all(parts, BOTH, 0, 0, tiled=True)
    coef = coef.reshape(n_wide, n_narrow, 2, mu_local // 2, 2 * ri_local)
    mu = n_narrow * mu_local
    packed = jax.ShapeDtypeStruct((mu, 2 * metric.shape[0]), BF16)
    part = jax.ShapeDtypeStruct((mu // 2, mu + 128), jnp.int16)
    packed, other = term_call(partner_kernel, "partner", (packed, part), core, coef, metric)
    other = lax.ppermute(other, "narrow", swap)
    total = jax.ShapeDtypeStruct((mu // 2, mu), F32)
    total = term_call(own_kernel, "own", total, core, packed, metric)
    parts = code_of(core, total, other, devices // 2)
    sides = [[j for j in range(devices) if j % 2 == c] for c in (0, 1)]
    got = lax.all_to_all(parts, BOTH, 0, 0, tiled=True, axis_index_groups=sides)
    return finish(me, got)


def solution(mesh):
    in_specs = (P("wide", "narrow", None), P("wide", "narrow", None), P("narrow", None), P())
    out_specs = P(("wide", "narrow"), None)
    return jax.shard_map(body, mesh=mesh, in_specs=in_specs, out_specs=out_specs, check_vma=False)
```
